32 devices in a mesh: space: 8 (over y, x, core), dp: 4 (over z).
Axes of the slice: x: 2, y: 2, z: 4, core: 2. Of those that a mesh axis runs over, the one named last changes fastest.
Arguments:
- block_in: bfloat16 [4, 8, 56, 56, 128], P('dp', 'space'), may hold values from -6 to 6
- weights: bfloat16 [3, 3, 128, 128], replicated, may hold values from -0.1875 to 0.1875
- out_bias: float32 [128], replicated, may hold values from -3 to 3
- adjacency: int32 [8, 8, 2], P('space'), may hold values from 0 to 7, as said below
- cotangent: bfloat16 [4, 8, 56, 56, 128], P('dp', 'space'), may hold values from -6 to 6
Outputs:
- block_out: bfloat16 [4, 8, 56, 56, 128], P('dp', 'space')
- weight_grad: float32 [3, 3, 128, 128], replicated
- grad_in: bfloat16 [4, 8, 56, 56, 128], P('dp', 'space')
The draws below stay inside these ranges and needn't reach their ends.
Inputs may be any that keep to these rules, and one draw needn't show every extreme that they name: adjacency[t, e] = (p, f) for e < 4 means that adjacency[p, f] = (t, e): edges are glued in pairs; entries 4 + k hold a tile and corner k' with adjacency[p, 4 + k'] = (t, k), corners glued in pairs. The corner pairing need not follow the edge pairing. Every edge and every corner of every tile appears exactly once as a partner. Column 1 lies in 0..3.
All inputs are finite; a program needn't handle non-finite values.
Results may differ from the reference program's by a relative error of at most 0.0031.
Values may be sent and summed in bfloat16 or wider, within the bound.
A program may use at most 64 MiB of HBM per device.

```python
import jax
import jax.numpy as jnp
from jax import lax

S = 56
C = 128
TILES = 8
BATCH = 4


def pair_up(key, slot_count):
    shuffled = jax.random.permutation(key, slot_count).astype(jnp.int32)
    partner = jnp.zeros((slot_count,), jnp.int32)
    partner = partner.at[shuffled[0::2]].set(shuffled[1::2])
    partner = partner.at[shuffled[1::2]].set(shuffled[0::2])
    return partner


def draw_adjacency(key, part):
    edge_mate = pair_up(jax.random.fold_in(key, 11), 4 * TILES)
    corner_mate = pair_up(jax.random.fold_in(key, 12), 4 * TILES)
    edge_part = jnp.stack([edge_mate // 4, edge_mate % 4], -1).reshape(TILES, 4, 2)
    corner_part = jnp.stack([corner_mate // 4, corner_mate % 4], -1).reshape(TILES, 4, 2)
    return jnp.concatenate([edge_part, corner_part], 1).astype(jnp.int32)


def block_scale(own_key, extent, shards, low, largest):
    def one(position, parts):
        steps = jax.random.uniform(jax.random.fold_in(jax.random.fold_in(own_key, 6), position), (parts,), jnp.float32, low / len(shards), largest / len(shards))
        return jnp.repeat(jnp.exp(steps), extent[position] // parts).reshape((-1,) + (1,) * (len(extent) - position - 1))

    factor_of = one(*shards[0])
    for cut in shards[1:]:
        factor_of = factor_of * one(*cut)
    return factor_of


def noise(rng, dims, spread, most, cuts=(), dtype=jnp.bfloat16):
    drawn = jax.random.normal(rng, dims, jnp.float32) * spread
    if len(cuts) > 0:
        drawn = block_scale(rng, dims, cuts, -0.22, 0.18) * drawn
    return jnp.clip(drawn, min=-most, max=most).astype(dtype)


def setup_inputs(seed: int = 0) -> dict:
    key_of = jax.random.split(jax.random.key(seed), 6)
    return {
        "block_in": noise(key_of[0], (BATCH, TILES, S, S, C), 1.0, 6.0, ((0, 4), (1, 8))),
        "weights": noise(key_of[1], (3, 3, C, C), (9 * C) ** -0.5, 0.1875),
        "out_bias": noise(key_of[2], (C,), 0.5, 3.0, (), jnp.float32),
        "adjacency": draw_adjacency(jax.random.fold_in(key_of[5], 71), 0),
        "cotangent": noise(key_of[4], (BATCH, TILES, S, S, C), 1.0, 6.0, ((0, 4), (1, 8))),
    }


def tile_edges(field):
    top_rim = field[..., 0, :, :]
    right_rim = field[..., :, -1, :]
    bottom_rim = jnp.flip(field[..., -1, :, :], -2)
    left_rim = jnp.flip(field[..., :, 0, :], -2)
    return jnp.stack([top_rim, right_rim, bottom_rim, left_rim], -3)


def tile_corners(field):
    return jnp.stack([field[..., 0, 0, :], field[..., 0, -1, :], field[..., -1, -1, :], field[..., -1, 0, :]], -2)


def assemble(field, near_edges, near_corners):
    top_row = jnp.concatenate([near_corners[0:1], jnp.flip(near_edges[0], 0), near_corners[1:2]], 0)
    bottom_row = jnp.concatenate([near_corners[3:4], near_edges[2], near_corners[2:3]], 0)
    middle = jnp.concatenate([near_edges[3][:, None], field, jnp.flip(near_edges[1], 0)[:, None]], 1)
    return jnp.concatenate([top_row[None], middle, bottom_row[None]], 0)


def conv_forward(padded, weights):
    side = padded.shape[0] - 2
    width = padded.shape[2]
    running = jnp.zeros((side * side, weights.shape[3]), jnp.float32)
    for row_off in range(3):
        for col_off in range(3):
            window = padded[row_off:row_off + side, col_off:col_off + side].reshape(side * side, width)
            running = running + jnp.dot(window, weights[row_off, col_off], preferred_element_type=jnp.float32)
    return running.reshape(side, side, -1)


def conv_backward(padded, grad_out, weights):
    side = padded.shape[0] - 2
    width = padded.shape[2]
    grad_rows = grad_out.reshape(side * side, -1)
    grad_pad = jnp.zeros(padded.shape, jnp.float32)
    kernel_rows = []
    for row_off in range(3):
        kernel_cols = []
        for col_off in range(3):
            window = padded[row_off:row_off + side, col_off:col_off + side].reshape(side * side, width)
            kernel_cols.append(jnp.dot(window.T, grad_rows, preferred_element_type=jnp.float32))
            back = jnp.dot(grad_rows, weights[row_off, col_off].T, preferred_element_type=jnp.float32)
            grad_pad = grad_pad + jnp.pad(back.reshape(side, side, width), ((row_off, 2 - row_off), (col_off, 2 - col_off), (0, 0)))
        kernel_rows.append(jnp.stack(kernel_cols, 0))
    return jnp.stack(kernel_rows, 0), grad_pad


def rim_grads(grad_pad):
    top_rim = grad_pad[0, 1:-1]
    right_rim = grad_pad[1:-1, -1]
    bottom_rim = jnp.flip(grad_pad[-1, 1:-1], 0)
    left_rim = jnp.flip(grad_pad[1:-1, 0], 0)
    rim_edges = jnp.stack([top_rim, right_rim, bottom_rim, left_rim], 0).astype(jnp.bfloat16)
    rim_corners = jnp.stack([grad_pad[0, 0], grad_pad[0, -1], grad_pad[-1, -1], grad_pad[-1, 0]], 0).astype(jnp.bfloat16)
    return rim_edges, rim_corners


def add_back(interior, back_edges, back_corners):
    edge_vals = back_edges.astype(jnp.float32)
    corner_vals = back_corners.astype(jnp.float32)
    interior = interior.at[0, :].add(jnp.flip(edge_vals[0], 0))
    interior = interior.at[:, -1].add(jnp.flip(edge_vals[1], 0))
    interior = interior.at[-1, :].add(edge_vals[2])
    interior = interior.at[:, 0].add(edge_vals[3])
    interior = interior.at[0, 0].add(corner_vals[0])
    interior = interior.at[0, -1].add(corner_vals[1])
    interior = interior.at[-1, -1].add(corner_vals[2])
    interior = interior.at[-1, 0].add(corner_vals[3])
    return interior


def reference(block_in, weights, out_bias, adjacency, cotangent):
    edge_tile = adjacency[:, 0:4, 0]
    edge_side = adjacency[:, 0:4, 1]
    corner_tile = adjacency[:, 4:8, 0]
    corner_side = adjacency[:, 4:8, 1]
    grad_acc = jnp.zeros(weights.shape, jnp.float32)
    results = []
    grads = []
    for sample in range(BATCH):
        inputs = block_in[sample]
        activation = jax.nn.silu(inputs.astype(jnp.float32)).astype(jnp.bfloat16)
        near_edges = tile_edges(activation)[edge_tile, edge_side]
        near_corners = tile_corners(activation)[corner_tile, corner_side]
        padded = jax.vmap(assemble)(activation, near_edges, near_corners)

        def tile_step(running, tile_items):
            pad_tile, tile_in, tile_cot = tile_items
            conv_sum = conv_forward(pad_tile, weights)
            result = (tile_in.astype(jnp.float32) + conv_sum + out_bias).astype(jnp.bfloat16)
            kernel_grad, grad_pad = conv_backward(pad_tile, tile_cot, weights)
            rim_edges, rim_corners = rim_grads(grad_pad)
            return running + kernel_grad, (result, grad_pad[1:-1, 1:-1], rim_edges, rim_corners)

        grad_acc, (result, interior, rim_edges, rim_corners) = lax.scan(tile_step, grad_acc, (padded, inputs, cotangent[sample]))
        back_edges = rim_edges[edge_tile, edge_side]
        back_corners = rim_corners[corner_tile, corner_side]
        act_grad = jax.vmap(add_back)(interior, back_edges, back_corners)
        input_f = inputs.astype(jnp.float32)
        sigmoid_x = jax.nn.sigmoid(input_f)
        grad_in = (cotangent[sample].astype(jnp.float32) + act_grad * sigmoid_x * (1.0 + input_f * (1.0 - sigmoid_x))).astype(jnp.bfloat16)
        results.append(result)
        grads.append(grad_in)
    return jnp.stack(results, 0), grad_acc, jnp.stack(grads, 0)
```

```python
import functools

import jax
import jax.numpy as jnp
from jax import lax
from jax.experimental import pallas as pl
from jax.experimental.pallas import tpu as pltpu
from jax.sharding import PartitionSpec as P

MESH = pl.DeviceIdType.MESH
ROWS = 8
F32 = jnp.float32
BF16 = jnp.bfloat16


def silu(v):
    return v / (1.0 + jnp.exp(-v))


def wide_of(side):
    return -(-(side + 4) // 16) * 16


def block_kernel(
    n_sp, n_dp, side,
    adj, x_in, w_in, bias, g_in,
    out, wg_out, gin_out,
    taps, gtaps, pad_grad, wt, acc, col_a, col_b, fwd, back, wg, parts, dps, full,
    fs, fr, bs, br, ss, sr, ds_, dr, gs, gr,
):
    wide = wide_of(side)
    chan = 128
    chunks = side // ROWS
    me = lax.axis_index("space")
    my_dp = lax.axis_index("dp")

    barrier = pltpu.get_barrier_semaphore()

    def greet_sp(k, c):
        pl.semaphore_signal(barrier, inc=1, device_id=(lax.rem(me + k, n_sp), my_dp), device_id_type=MESH)
        return c

    def greet_dp(k, c):
        pl.semaphore_signal(barrier, inc=1, device_id=(me, lax.rem(my_dp + k, n_dp)), device_id_type=MESH)
        return c

    lax.fori_loop(1, n_sp, greet_sp, 0)
    lax.fori_loop(1, n_dp, greet_dp, 0)

    def at_sp(k):
        peer = lax.rem(me + k, n_sp)
        return peer, (peer, my_dp)

    def at_dp(k):
        peer = lax.rem(my_dp + k, n_dp)
        return peer, (me, peer)

    def gather_copy(buf, mine, where, send, recv, k):
        peer, dev = where(k)
        start = pltpu.make_async_remote_copy(
            src_ref=buf.at[mine], dst_ref=buf.at[mine], send_sem=send.at[peer],
            recv_sem=recv.at[mine], device_id=dev, device_id_type=MESH)
        wait = pltpu.make_async_remote_copy(
            src_ref=buf.at[mine], dst_ref=buf.at[peer], send_sem=send.at[peer],
            recv_sem=recv.at[peer], device_id=dev, device_id_type=MESH)
        return start, wait

    def begin(buf, mine, n, where, send, recv):
        def go(k, c):
            gather_copy(buf, mine, where, send, recv, k)[0].start()
            return c
        lax.fori_loop(1, n, go, 0)

    def finish(buf, mine, n, where, send, recv):
        def go(k, c):
            gather_copy(buf, mine, where, send, recv, k)[1].wait()
            return c
        lax.fori_loop(1, n, go, 0)

    r64 = lax.broadcasted_iota(jnp.int32, (wide, chan), 0)
    ra = lax.broadcasted_iota(jnp.int32, (wide, wide), 0)
    rb = lax.broadcasted_iota(jnp.int32, (wide, wide), 1)
    mirror = jnp.where(ra + rb == side - 1, 1.0, 0.0).astype(BF16)

    def flip(v):
        return jnp.dot(mirror, v, preferred_element_type=F32)

    s8 = lax.broadcasted_iota(jnp.int32, (ROWS, 8, chan), 1)

    def column(block, at):
        return jnp.sum(jnp.where(s8 == at, block, 0.0), axis=1)

    tail = jnp.zeros((wide - side, chan), F32)

    def widen(v):
        return jnp.concatenate([v, tail], axis=0)

    for c in range(chunks):
        lo = c * ROWS
        left = x_in[lo:lo + ROWS, 0:8, :].astype(F32)
        right = x_in[lo:lo + ROWS, side - 8:side, :].astype(F32)
        col_a[lo:lo + ROWS, :] = silu(column(left, 0))
        col_b[lo:lo + ROWS, :] = silu(column(right, 7))
    col_a[side:wide, :] = tail
    col_b[side:wide, :] = tail
    fwd[me, 0] = widen(silu(x_in[0].astype(F32))).astype(BF16)
    fwd[me, 1] = col_b[...].astype(BF16)
    fwd[me, 2] = flip(widen(silu(x_in[side - 1].astype(F32))).astype(BF16)).astype(BF16)
    fwd[me, 3] = flip(col_a[...].astype(BF16)).astype(BF16)
    pl.semaphore_wait(barrier, n_sp + n_dp - 2)
    begin(fwd, me, n_sp, at_sp, fs, fr)

    for r in range(3):
        for c in range(3):
            block = w_in[2 - r, (2 - c) * chan:(3 - c) * chan, :].astype(F32)
            wt[r, c * chan:(c + 1) * chan, :] = block.T.astype(BF16)
    zero_row = jnp.zeros((wide, 3 * chan), BF16)
    for row in (0, 1, side + 2, side + 3):
        gtaps[row] = zero_row

    def spread_grad(c, carry):
        for k in range(ROWS):
            i = c * ROWS + k
            g = widen(g_in[i].astype(F32))
            gtaps[i + 2, :, 0:chan] = pltpu.roll(g, 2, 0).astype(BF16)
            gtaps[i + 2, :, chan:2 * chan] = pltpu.roll(g, 1, 0).astype(BF16)
            gtaps[i + 2, :, 2 * chan:] = g.astype(BF16)
        return carry

    lax.fori_loop(0, chunks, spread_grad, 0)

    def grad_rows(first, count):
        total = jnp.zeros((count * wide, chan), F32)
        for r in range(3):
            total += jnp.dot(
                gtaps[pl.ds(first + r, count)].reshape(count * wide, 3 * chan), wt[r],
                preferred_element_type=F32)
        pad_grad[pl.ds(first, count)] = total.reshape(count, wide, chan)

    def grad_chunk(c, carry):
        grad_rows(c * ROWS, ROWS)
        return carry

    lax.fori_loop(0, chunks, grad_chunk, 0)
    grad_rows(side, 2)

    for c in range(chunks):
        lo = c * ROWS
        col_a[lo:lo + ROWS, :] = column(pad_grad[lo + 1:lo + 1 + ROWS, 0:8, :], 0)
        col_b[lo:lo + ROWS, :] = column(pad_grad[lo + 1:lo + 1 + ROWS, side:side + 8, :], 1)
    first_row = pad_grad[0]
    last_row = pad_grad[side + 1]
    top = pltpu.roll(first_row, wide - 1, 0)
    bottom = pltpu.roll(last_row, wide - 1, 0)

    def pack(v, corner):
        return jnp.where(r64 < side, v, jnp.where(r64 == side, corner, 0.0)).astype(BF16)

    back[me, 0] = pack(top, first_row[0:1])
    back[me, 1] = pack(col_b[...], first_row[side + 1:side + 2])
    back[me, 2] = pack(flip(bottom.astype(BF16)), last_row[side + 1:side + 2])
    back[me, 3] = pack(flip(col_a[...].astype(BF16)), last_row[0:1])
    begin(back, me, n_sp, at_sp, bs, br)

    def put_taps(row, a):
        taps[row, :, 0:chan] = pltpu.roll(a, 1, 0).astype(BF16)
        taps[row, :, chan:2 * chan] = a.astype(BF16)
        taps[row, :, 2 * chan:] = pltpu.roll(a, wide - 1, 0).astype(BF16)

    def spread_act(c, carry):
        for k in range(ROWS):
            i = c * ROWS + k
            put_taps(i + 1, widen(silu(x_in[i].astype(F32))))
        return carry

    lax.fori_loop(0, chunks, spread_act, 0)
    finish(fwd, me, n_sp, at_sp, fs, fr)

    def near(buf, e):
        return buf[adj[0, e, 0], adj[0, e, 1]]

    def near_corner(buf, k, row):
        return buf[adj[0, 4 + k, 0], adj[0, 4 + k, 1]].astype(F32)[row:row + 1]

    corner = [near_corner(fwd, k, 0) for k in range(4)]

    def rim_row(v, behind, ahead):
        return jnp.where(r64 < side, v, jnp.where(r64 == side, behind, jnp.where(r64 == wide - 1, ahead, 0.0)))

    put_taps(0, rim_row(flip(near(fwd, 0)), corner[1], corner[0]))
    put_taps(side + 1, rim_row(near(fwd, 2).astype(F32), corner[2], corner[3]))
    col_a[...] = near(fwd, 3).astype(F32)
    col_b[...] = flip(near(fwd, 1))
    s16 = lax.broadcasted_iota(jnp.int32, (ROWS, 16, chan), 1)
    at_right = (side - 1) // 16 * 16
    for c in range(chunks):
        lo = c * ROWS
        v = taps[lo + 1:lo + 1 + ROWS, 0:16, 0:chan].astype(F32)
        v = jnp.where(s16 == 0, col_a[lo:lo + ROWS, :][:, None, :], v)
        taps[lo + 1:lo + 1 + ROWS, 0:16, 0:chan] = v.astype(BF16)
        v = taps[lo + 1:lo + 1 + ROWS, at_right:at_right + 16, 2 * chan:].astype(F32)
        v = jnp.where(s16 == side - 1 - at_right, col_b[lo:lo + ROWS, :][:, None, :], v)
        taps[lo + 1:lo + 1 + ROWS, at_right:at_right + 16, 2 * chan:] = v.astype(BF16)

    acc[...] = jnp.zeros_like(acc)

    def kernel_chunk(c, carry):
        i0 = c * ROWS
        gt = gtaps[pl.ds(i0 + 2, ROWS), :, 2 * chan:].reshape(ROWS * wide, chan).T
        for r in range(3):
            acc[r] += jnp.dot(
                gt, taps[pl.ds(i0 + r, ROWS)].reshape(ROWS * wide, 3 * chan),
                preferred_element_type=F32)
        return carry

    lax.fori_loop(0, chunks, kernel_chunk, 0)
    for r in range(3):
        for c in range(3):
            at = (3 * r + c) * chan
            wg[at:at + chan, :] = acc[r, :, c * chan:(c + 1) * chan].T.astype(BF16)
    size = parts.shape[1]
    used = 9 * chan
    if n_sp * size > used:
        wg[used:, :] = jnp.zeros((n_sp * size - used, chan), BF16)

    def scatter_copy(k):
        peer, dev = at_sp(k)
        src = wg.at[pl.ds(pl.multiple_of(peer * size, 16), size)]
        start = pltpu.make_async_remote_copy(
            src_ref=src, dst_ref=parts.at[me], send_sem=ss.at[peer],
            recv_sem=sr.at[me], device_id=dev, device_id_type=MESH)
        wait = pltpu.make_async_remote_copy(
            src_ref=src, dst_ref=parts.at[peer], send_sem=ss.at[peer],
            recv_sem=sr.at[peer], device_id=dev, device_id_type=MESH)
        return start, wait

    def scatter_start(k, c):
        scatter_copy(k)[0].start()
        return c

    def scatter_wait(k, c):
        scatter_copy(k)[1].wait()
        return c

    lax.fori_loop(1, n_sp, scatter_start, 0)
    parts[me] = wg[pl.ds(pl.multiple_of(me * size, 16), size), :]

    def conv_chunk(c, carry):
        i0 = c * ROWS
        total = jnp.zeros((ROWS * wide, chan), F32)
        for r in range(3):
            total += jnp.dot(
                taps[pl.ds(i0 + r, ROWS)].reshape(ROWS * wide, 3 * chan), w_in[r],
                preferred_element_type=F32)
        conv = total.reshape(ROWS, wide, chan)[:, :side, :]
        field = x_in[pl.ds(i0, ROWS)].astype(F32)
        out[pl.ds(i0, ROWS)] = (field + conv + bias[...].reshape(1, 1, chan)).astype(BF16)
        return carry

    lax.fori_loop(0, chunks, conv_chunk, 0)

    lax.fori_loop(1, n_sp, scatter_wait, 0)
    mine = lax.fori_loop(0, n_sp, lambda k, t: t + parts[k].astype(F32), jnp.zeros((size, chan), F32))
    dps[my_dp] = mine.astype(BF16)
    begin(dps, my_dp, n_dp, at_dp, ds_, dr)

    finish(back, me, n_sp, at_sp, bs, br)

    def inner(v):
        return jnp.where(r64 < side, v, 0.0)

    ends = [near_corner(back, k, side) for k in range(4)]
    pad_grad[1] += pltpu.roll(inner(flip(near(back, 0))), 1, 0)
    pad_grad[side] += pltpu.roll(inner(near(back, 2).astype(F32)), 1, 0)
    col_a[...] = inner(near(back, 3).astype(F32)) + jnp.where(r64 == 0, ends[0], jnp.where(r64 == side - 1, ends[3], 0.0))
    col_b[...] = inner(flip(near(back, 1))) + jnp.where(r64 == 0, ends[1], jnp.where(r64 == side - 1, ends[2], 0.0))

    r56 = lax.broadcasted_iota(jnp.int32, (side, chan), 0)

    def finish_rows(c, carry):
        for k in range(ROWS):
            i = c * ROWS + k
            p = pltpu.roll(pad_grad[i + 1], wide - 1, 0)[:side]
            p = p + jnp.where(r56 == 0, col_a[pl.ds(i, 1), :], jnp.where(r56 == side - 1, col_b[pl.ds(i, 1), :], 0.0))
            v = x_in[i].astype(F32)
            s = 1.0 / (1.0 + jnp.exp(-v))
            gin_out[i] = (g_in[i].astype(F32) + p * s * (1.0 + v * (1.0 - s))).astype(BF16)
        return carry

    lax.fori_loop(0, chunks, finish_rows, 0)

    finish(dps, my_dp, n_dp, at_dp, ds_, dr)
    total = dps[0].astype(F32)
    for d in range(1, n_dp):
        total = total + dps[d].astype(F32)
    full[me] = total.astype(BF16)
    begin(full, me, n_sp, at_sp, gs, gr)
    finish(full, me, n_sp, at_sp, gs, gr)
    if n_sp * size > used:
        wg_out[...] = full[...].astype(F32).reshape(n_sp * size, chan)[:used]
    else:
        wg_out[...] = full[...].astype(F32).reshape(n_sp * size, chan)


def per_device(n_sp, n_dp, block_in, weights, out_bias, adjacency, cotangent):
    side, chan = block_in.shape[2], block_in.shape[4]
    wide = wide_of(side)
    size = -(-9 * chan // (16 * n_sp)) * 16
    vmem = pl.BlockSpec(memory_space=pltpu.VMEM)
    sem = pltpu.SemaphoreType.DMA
    result, wgrad, grad_in = pl.pallas_call(
        functools.partial(block_kernel, n_sp, n_dp, side),
        out_shape=(
            jax.ShapeDtypeStruct((side, side, chan), BF16),
            jax.ShapeDtypeStruct((9 * chan, chan), F32),
            jax.ShapeDtypeStruct((side, side, chan), BF16),
        ),
        in_specs=[pl.BlockSpec(memory_space=pltpu.SMEM), vmem, vmem, vmem, vmem],
        out_specs=(vmem, vmem, vmem),
        scratch_shapes=[
            pltpu.VMEM((side + 2, wide, 3 * chan), BF16),
            pltpu.VMEM((side + 4, wide, 3 * chan), BF16),
            pltpu.VMEM((side + 2, wide, chan), F32),
            pltpu.VMEM((3, 3 * chan, chan), BF16),
            pltpu.VMEM((3, chan, 3 * chan), F32),
            pltpu.VMEM((wide, chan), F32),
            pltpu.VMEM((wide, chan), F32),
            pltpu.VMEM((n_sp, 4, wide, chan), BF16),
            pltpu.VMEM((n_sp, 4, wide, chan), BF16),
            pltpu.VMEM((n_sp * size, chan), BF16),
            pltpu.VMEM((n_sp, size, chan), BF16),
            pltpu.VMEM((n_dp, size, chan), BF16),
            pltpu.VMEM((n_sp, size, chan), BF16),
            sem((n_sp,)), sem((n_sp,)), sem((n_sp,)), sem((n_sp,)), sem((n_sp,)), sem((n_sp,)),
            sem((n_dp,)), sem((n_dp,)), sem((n_sp,)), sem((n_sp,)),
        ],
        compiler_params=pltpu.CompilerParams(
            collective_id=0, has_side_effects=True, vmem_limit_bytes=56 * 2**20),
    )(
        adjacency, block_in[0, 0], weights.reshape(3, 3 * chan, chan), out_bias.reshape(1, chan),
        cotangent[0, 0],
    )
    return (result[None, None], wgrad.reshape(weights.shape), grad_in[None, None])


def solution(mesh):
    placed = (
        P("dp", "space", None, None, None),
        P(),
        P(),
        P("space", None, None),
        P("dp", "space", None, None, None),
    )
    return jax.shard_map(
        functools.partial(per_device, mesh.shape["space"], mesh.shape["dp"]),
        mesh=mesh,
        in_specs=placed,
        out_specs=(P("dp", "space", None, None, None), P(), P("dp", "space", None, None, None)),
        check_vma=False,
    )
```

```python
import functools

import jax
import jax.numpy as jnp
from jax import lax
from jax.experimental import pallas as pl
from jax.experimental.pallas import tpu as pltpu
from jax.sharding import PartitionSpec as P

MESH = pl.DeviceIdType.MESH
ROWS = 8
F32 = jnp.float32
BF16 = jnp.bfloat16


def silu(v):
    return v / (1.0 + jnp.exp(-v))


def encode(v):
    top = jnp.maximum(jnp.max(jnp.abs(v), axis=0, keepdims=True), 1e-30)
    power = jnp.ceil(jnp.log2(top))
    code = jnp.clip(jnp.round(v * jnp.exp2(15.0 - power)), -32767.0, 32767.0)
    rows = jnp.concatenate([code, jnp.broadcast_to(power, (16, v.shape[1]))], axis=0)
    return rows.astype(jnp.int32).astype(jnp.int16)


def decode(rows):
    v = rows.astype(jnp.int32).astype(F32)
    size = v.shape[0] - 16
    return v[:size] * jnp.exp2(v[size:size + 1] - 15.0)


def wide_of(side):
    return -(-(side + 4) // 16) * 16


def block_kernel(
    n_sp, n_dp, side,
    adj, x_in, w_in, bias, g_in,
    out_hbm, wg_out, gin_hbm,
    taps, gtaps, pad_grad, wt, acc, col_a, col_b, fwd, back, wg, parts, dps, full,
    fs, fr, bs, br, ss, sr, ds_, dr, gs, gr, out, gin_out, wgf, lo_sem,
):
    wide = wide_of(side)
    chan = 128
    chunks = side // ROWS
    me = lax.axis_index("space")
    my_dp = lax.axis_index("dp")

    barrier = pltpu.get_barrier_semaphore()

    def greet_sp(k, c):
        pl.semaphore_signal(barrier, inc=1, device_id=(lax.rem(me + k, n_sp), my_dp), device_id_type=MESH)
        return c

    def greet_dp(k, c):
        pl.semaphore_signal(barrier, inc=1, device_id=(me, lax.rem(my_dp + k, n_dp)), device_id_type=MESH)
        return c

    lax.fori_loop(1, n_sp, greet_sp, 0)
    lax.fori_loop(1, n_dp, greet_dp, 0)

    def at_sp(k):
        peer = lax.rem(me + k, n_sp)
        return peer, (peer, my_dp)

    def at_dp(k):
        peer = lax.rem(my_dp + k, n_dp)
        return peer, (me, peer)

    def gather_copy(buf, mine, where, send, recv, k):
        peer, dev = where(k)
        start = pltpu.make_async_remote_copy(
            src_ref=buf.at[mine], dst_ref=buf.at[mine], send_sem=send.at[peer],
            recv_sem=recv.at[mine], device_id=dev, device_id_type=MESH)
        wait = pltpu.make_async_remote_copy(
            src_ref=buf.at[mine], dst_ref=buf.at[peer], send_sem=send.at[peer],
            recv_sem=recv.at[peer], device_id=dev, device_id_type=MESH)
        return start, wait

    def begin(buf, mine, n, where, send, recv):
        def go(k, c):
            gather_copy(buf, mine, where, send, recv, k)[0].start()
            return c
        lax.fori_loop(1, n, go, 0)

    def finish(buf, mine, n, where, send, recv):
        def go(k, c):
            gather_copy(buf, mine, where, send, recv, k)[1].wait()
            return c
        lax.fori_loop(1, n, go, 0)

    r64 = lax.broadcasted_iota(jnp.int32, (wide, chan), 0)
    ra = lax.broadcasted_iota(jnp.int32, (wide, wide), 0)
    rb = lax.broadcasted_iota(jnp.int32, (wide, wide), 1)
    mirror = jnp.where(ra + rb == side - 1, 1.0, 0.0).astype(BF16)

    def flip(v):
        return jnp.dot(mirror, v, preferred_element_type=F32)

    s8 = lax.broadcasted_iota(jnp.int32, (ROWS, 8, chan), 1)

    def column(block, at):
        return jnp.sum(jnp.where(s8 == at, block, 0.0), axis=1)

    tail = jnp.zeros((wide - side, chan), F32)

    def widen(v):
        return jnp.concatenate([v, tail], axis=0)

    for c in range(chunks):
        lo = c * ROWS
        left = x_in[lo:lo + ROWS, 0:8, :].astype(F32)
        right = x_in[lo:lo + ROWS, side - 8:side, :].astype(F32)
        col_a[lo:lo + ROWS, :] = silu(column(left, 0))
        col_b[lo:lo + ROWS, :] = silu(column(right, 7))
    col_a[side:wide, :] = tail
    col_b[side:wide, :] = tail
    fwd[me, 0] = widen(silu(x_in[0].astype(F32))).astype(BF16)
    fwd[me, 1] = col_b[...].astype(BF16)
    fwd[me, 2] = flip(widen(silu(x_in[side - 1].astype(F32))).astype(BF16)).astype(BF16)
    fwd[me, 3] = flip(col_a[...].astype(BF16)).astype(BF16)
    pl.semaphore_wait(barrier, n_sp + n_dp - 2)
    begin(fwd, me, n_sp, at_sp, fs, fr)

    for r in range(3):
        for c in range(3):
            block = w_in[2 - r, (2 - c) * chan:(3 - c) * chan, :].astype(F32)
            wt[r, c * chan:(c + 1) * chan, :] = block.T.astype(BF16)
    zero_row = jnp.zeros((wide, 3 * chan), BF16)
    for row in (0, 1, side + 2, side + 3):
        gtaps[row] = zero_row

    def spread_grad(c, carry):
        for k in range(ROWS):
            i = c * ROWS + k
            g = widen(g_in[i].astype(F32))
            gtaps[i + 2, :, 0:chan] = pltpu.roll(g, 2, 0).astype(BF16)
            gtaps[i + 2, :, chan:2 * chan] = pltpu.roll(g, 1, 0).astype(BF16)
            gtaps[i + 2, :, 2 * chan:] = g.astype(BF16)
        return carry

    lax.fori_loop(0, chunks, spread_grad, 0)

    def grad_rows(first, count):
        total = jnp.zeros((count * wide, chan), F32)
        for r in range(3):
            total += jnp.dot(
                gtaps[pl.ds(first + r, count)].reshape(count * wide, 3 * chan), wt[r],
                preferred_element_type=F32)
        pad_grad[pl.ds(first, count)] = total.reshape(count, wide, chan)

    def grad_chunk(c, carry):
        grad_rows(c * ROWS, ROWS)
        return carry

    lax.fori_loop(0, chunks, grad_chunk, 0)
    grad_rows(side, 2)

    for c in range(chunks):
        lo = c * ROWS
        col_a[lo:lo + ROWS, :] = column(pad_grad[lo + 1:lo + 1 + ROWS, 0:8, :], 0)
        col_b[lo:lo + ROWS, :] = column(pad_grad[lo + 1:lo + 1 + ROWS, side:side + 8, :], 1)
    first_row = pad_grad[0]
    last_row = pad_grad[side + 1]
    top = pltpu.roll(first_row, wide - 1, 0)
    bottom = pltpu.roll(last_row, wide - 1, 0)

    def pack(v, corner):
        return jnp.where(r64 < side, v, jnp.where(r64 == side, corner, 0.0)).astype(BF16)

    back[me, 0] = pack(top, first_row[0:1])
    back[me, 1] = pack(col_b[...], first_row[side + 1:side + 2])
    back[me, 2] = pack(flip(bottom.astype(BF16)), last_row[side + 1:side + 2])
    back[me, 3] = pack(flip(col_a[...].astype(BF16)), last_row[0:1])

    def put_taps(row, a):
        taps[row, :, 0:chan] = pltpu.roll(a, 1, 0).astype(BF16)
        taps[row, :, chan:2 * chan] = a.astype(BF16)
        taps[row, :, 2 * chan:] = pltpu.roll(a, wide - 1, 0).astype(BF16)

    def spread_act(c, carry):
        for k in range(ROWS):
            i = c * ROWS + k
            put_taps(i + 1, widen(silu(x_in[i].astype(F32))))
        return carry

    lax.fori_loop(0, chunks, spread_act, 0)
    finish(fwd, me, n_sp, at_sp, fs, fr)

    def near(buf, e):
        return buf[adj[0, 0, e], adj[0, 1, e]]

    def near_corner(buf, k, row):
        return buf[adj[0, 0, 4 + k], adj[0, 1, 4 + k]].astype(F32)[row:row + 1]

    corner = [near_corner(fwd, k, 0) for k in range(4)]

    def rim_row(v, behind, ahead):
        return jnp.where(r64 < side, v, jnp.where(r64 == side, behind, jnp.where(r64 == wide - 1, ahead, 0.0)))

    put_taps(0, rim_row(flip(near(fwd, 0)), corner[1], corner[0]))
    put_taps(side + 1, rim_row(near(fwd, 2).astype(F32), corner[2], corner[3]))
    col_a[...] = near(fwd, 3).astype(F32)
    col_b[...] = flip(near(fwd, 1))
    s16 = lax.broadcasted_iota(jnp.int32, (ROWS, 16, chan), 1)
    at_right = (side - 1) // 16 * 16
    for c in range(chunks):
        lo = c * ROWS
        v = taps[lo + 1:lo + 1 + ROWS, 0:16, 0:chan].astype(F32)
        v = jnp.where(s16 == 0, col_a[lo:lo + ROWS, :][:, None, :], v)
        taps[lo + 1:lo + 1 + ROWS, 0:16, 0:chan] = v.astype(BF16)
        v = taps[lo + 1:lo + 1 + ROWS, at_right:at_right + 16, 2 * chan:].astype(F32)
        v = jnp.where(s16 == side - 1 - at_right, col_b[lo:lo + ROWS, :][:, None, :], v)
        taps[lo + 1:lo + 1 + ROWS, at_right:at_right + 16, 2 * chan:] = v.astype(BF16)

    acc[...] = jnp.zeros_like(acc)

    def kernel_chunk(c, carry):
        i0 = c * ROWS
        gt = gtaps[pl.ds(i0 + 2, ROWS), :, 2 * chan:].reshape(ROWS * wide, chan).T
        for r in range(3):
            acc[r] += jnp.dot(
                gt, taps[pl.ds(i0 + r, ROWS)].reshape(ROWS * wide, 3 * chan),
                preferred_element_type=F32)
        return carry

    lax.fori_loop(0, chunks, kernel_chunk, 0)
    for r in range(3):
        for c in range(3):
            at = (3 * r + c) * chan
            wgf[at:at + chan, :] = acc[r, :, c * chan:(c + 1) * chan].T
    size = parts.shape[1] - 16
    used = 9 * chan
    if n_sp * size > used:
        wgf[used:, :] = jnp.zeros((n_sp * size - used, chan), F32)

    def scatter_copy(k):
        peer, dev = at_sp(k)
        src = wg.at[peer]
        start = pltpu.make_async_remote_copy(
            src_ref=src, dst_ref=parts.at[me], send_sem=ss.at[peer],
            recv_sem=sr.at[me], device_id=dev, device_id_type=MESH)
        wait = pltpu.make_async_remote_copy(
            src_ref=src, dst_ref=parts.at[peer], send_sem=ss.at[peer],
            recv_sem=sr.at[peer], device_id=dev, device_id_type=MESH)
        return start, wait

    def own_rows(peer):
        return wgf[pl.ds(pl.multiple_of(peer * size, 16), size), :]

    def scatter_start(k, c):
        peer = lax.rem(me + k, n_sp)
        wg[peer] = encode(own_rows(peer))
        scatter_copy(k)[0].start()
        return c

    def scatter_wait(k, c):
        scatter_copy(k)[1].wait()
        return c

    lax.fori_loop(1, n_sp, scatter_start, 0)
    parts[me] = encode(own_rows(me))
    begin(back, me, n_sp, at_sp, bs, br)

    def conv_chunk(c, carry):
        i0 = c * ROWS
        total = jnp.zeros((ROWS * wide, chan), F32)
        for r in range(3):
            total += jnp.dot(
                taps[pl.ds(i0 + r, ROWS)].reshape(ROWS * wide, 3 * chan), w_in[r],
                preferred_element_type=F32)
        conv = total.reshape(ROWS, wide, chan)[:, :side, :]
        field = x_in[pl.ds(i0, ROWS)].astype(F32)
        out[pl.ds(i0, ROWS)] = (field + conv + bias[...].reshape(1, 1, chan)).astype(BF16)
        return carry

    lax.fori_loop(0, chunks, conv_chunk, 0)
    out_copy = pltpu.make_async_copy(out, out_hbm, lo_sem.at[0])
    out_copy.start()

    lax.fori_loop(1, n_sp, scatter_wait, 0)
    mine = lax.fori_loop(0, n_sp, lambda k, t: t + decode(parts[k]), jnp.zeros((size, chan), F32))
    dps[my_dp] = encode(mine)
    begin(dps, my_dp, n_dp, at_dp, ds_, dr)

    finish(back, me, n_sp, at_sp, bs, br)

    def inner(v):
        return jnp.where(r64 < side, v, 0.0)

    ends = [near_corner(back, k, side) for k in range(4)]
    pad_grad[1] += pltpu.roll(inner(flip(near(back, 0))), 1, 0)
    pad_grad[side] += pltpu.roll(inner(near(back, 2).astype(F32)), 1, 0)
    col_a[...] = inner(near(back, 3).astype(F32)) + jnp.where(r64 == 0, ends[0], jnp.where(r64 == side - 1, ends[3], 0.0))
    col_b[...] = inner(flip(near(back, 1))) + jnp.where(r64 == 0, ends[1], jnp.where(r64 == side - 1, ends[2], 0.0))

    r56 = lax.broadcasted_iota(jnp.int32, (side, chan), 0)

    def finish_rows(c, carry):
        for k in range(ROWS):
            i = c * ROWS + k
            p = pltpu.roll(pad_grad[i + 1], wide - 1, 0)[:side]
            p = p + jnp.where(r56 == 0, col_a[pl.ds(i, 1), :], jnp.where(r56 == side - 1, col_b[pl.ds(i, 1), :], 0.0))
            v = x_in[i].astype(F32)
            s = 1.0 / (1.0 + jnp.exp(-v))
            gin_out[i] = (g_in[i].astype(F32) + p * s * (1.0 + v * (1.0 - s))).astype(BF16)
        return carry

    lax.fori_loop(0, chunks, finish_rows, 0)
    gin_copy = pltpu.make_async_copy(gin_out, gin_hbm, lo_sem.at[1])
    gin_copy.start()

    finish(dps, my_dp, n_dp, at_dp, ds_, dr)
    total = decode(dps[0])
    for d in range(1, n_dp):
        total = total + decode(dps[d])
    full[me] = encode(total)
    begin(full, me, n_sp, at_sp, gs, gr)
    finish(full, me, n_sp, at_sp, gs, gr)
    def open_rows(k, c):
        wgf[pl.ds(pl.multiple_of(k * size, 16), size), :] = decode(full[k])
        return c

    lax.fori_loop(0, n_sp, open_rows, 0)
    kernel_copy = pltpu.make_async_copy(wgf.at[pl.ds(0, used)], wg_out, lo_sem.at[2])
    kernel_copy.start()
    kernel_copy.wait()
    gin_copy.wait()
    out_copy.wait()


def hand_on(*refs):
    count = len(refs) // 2
    sems = refs[-1]
    copies = [pltpu.make_async_copy(refs[k], refs[count + k], sems.at[k]) for k in range(count)]
    for one in copies:
        one.start()
    for one in copies:
        one.wait()


def per_device(n_sp, n_dp, block_in, weights, out_bias, adjacency, cotangent):
    side, chan = block_in.shape[2], block_in.shape[4]
    wide = wide_of(side)
    size = -(-9 * chan // (16 * n_sp)) * 16
    vmem = pl.BlockSpec(memory_space=pltpu.VMEM)
    hbm = pl.BlockSpec(memory_space=pl.ANY)
    sem = pltpu.SemaphoreType.DMA
    shapes = (
        jax.ShapeDtypeStruct((side, side, chan), BF16),
        jax.ShapeDtypeStruct((9 * chan, chan), F32),
        jax.ShapeDtypeStruct((side, side, chan), BF16),
    )
    held = pl.pallas_call(
        functools.partial(block_kernel, n_sp, n_dp, side),
        out_shape=shapes,
        in_specs=[pl.BlockSpec(memory_space=pltpu.SMEM), vmem, vmem, vmem, vmem],
        out_specs=(hbm, hbm, hbm),
        scratch_shapes=[
            pltpu.VMEM((side + 2, wide, 3 * chan), BF16),
            pltpu.VMEM((side + 4, wide, 3 * chan), BF16),
            pltpu.VMEM((side + 2, wide, chan), F32),
            pltpu.VMEM((3, 3 * chan, chan), BF16),
            pltpu.VMEM((3, chan, 3 * chan), F32),
            pltpu.VMEM((wide, chan), F32),
            pltpu.VMEM((wide, chan), F32),
            pltpu.VMEM((n_sp, 4, wide, chan), BF16),
            pltpu.VMEM((n_sp, 4, wide, chan), BF16),
            pltpu.VMEM((n_sp, size + 16, chan), jnp.int16),
            pltpu.VMEM((n_sp, size + 16, chan), jnp.int16),
            pltpu.VMEM((n_dp, size + 16, chan), jnp.int16),
            pltpu.VMEM((n_sp, size + 16, chan), jnp.int16),
            sem((n_sp,)), sem((n_sp,)), sem((n_sp,)), sem((n_sp,)), sem((n_sp,)), sem((n_sp,)),
            sem((n_dp,)), sem((n_dp,)), sem((n_sp,)), sem((n_sp,)),
            pltpu.VMEM((side, side, chan), BF16),
            pltpu.VMEM((side, side, chan), BF16),
            pltpu.VMEM((n_sp * size, chan), F32),
            sem((3,)),
        ],
        compiler_params=pltpu.CompilerParams(
            collective_id=0, has_side_effects=True, vmem_limit_bytes=56 * 2**20),
    )(
        adjacency.transpose(0, 2, 1), block_in[0, 0], weights.reshape(3, 3 * chan, chan), out_bias.reshape(1, chan),
        cotangent[0, 0],
    )
    result, wgrad, grad_in = pl.pallas_call(
        hand_on,
        out_shape=shapes,
        in_specs=[hbm, hbm, hbm],
        out_specs=(hbm, hbm, hbm),
        scratch_shapes=[sem((3,))],
    )(*held)
    return (result[None, None], wgrad.reshape(weights.shape), grad_in[None, None])


def solution(mesh):
    placed = (
        P("dp", "space", None, None, None),
        P(),
        P(),
        P("space", None, None),
        P("dp", "space", None, None, None),
    )
    return jax.shard_map(
        functools.partial(per_device, mesh.shape["space"], mesh.shape["dp"]),
        mesh=mesh,
        in_specs=placed,
        out_specs=(P("dp", "space", None, None, None), P(), P("dp", "space", None, None, None)),
        check_vma=False,
    )
```

```python
import functools

import jax
import jax.numpy as jnp
from jax import lax
from jax.experimental import pallas as pl
from jax.experimental.pallas import tpu as pltpu
from jax.sharding import PartitionSpec as P

MESH = pl.DeviceIdType.MESH
ROWS = 8
F32 = jnp.float32
BF16 = jnp.bfloat16


def silu(v):
    return v / (1.0 + jnp.exp(-v))


def encode(v):
    top = jnp.maximum(jnp.max(jnp.abs(v), axis=0, keepdims=True), 1e-30)
    power = jnp.ceil(jnp.log2(top))
    code = jnp.clip(jnp.round(v * jnp.exp2(15.0 - power)), -32767.0, 32767.0)
    rows = jnp.concatenate([code, jnp.broadcast_to(power, (16, v.shape[1]))], axis=0)
    return rows.astype(jnp.int32).astype(jnp.int16)


def decode(rows):
    v = rows.astype(jnp.int32).astype(F32)
    size = v.shape[0] - 16
    return v[:size] * jnp.exp2(v[size:size + 1] - 15.0)


def wide_of(side):
    return -(-(side + 4) // 16) * 16


def block_kernel(
    n_sp, n_dp, side,
    adj, x_in, w_in, bias, g_in,
    out_hbm, wg_out, gin_hbm,
    taps, gtaps, pad_grad, wt, acc, col_a, col_b, fwd, back, wg, parts, dps, full,
    fs, fr, bs, br, ss, sr, ds_, dr, gs, gr, out, gin_out, wgf, lo_sem, col_g,
):
    wide = wide_of(side)
    chan = 128
    chunks = side // ROWS
    me = lax.axis_index("space")
    my_dp = lax.axis_index("dp")

    barrier = pltpu.get_barrier_semaphore()

    def greet_sp(k, c):
        pl.semaphore_signal(barrier, inc=1, device_id=(lax.rem(me + k, n_sp), my_dp), device_id_type=MESH)
        return c

    def greet_dp(k, c):
        pl.semaphore_signal(barrier, inc=1, device_id=(me, lax.rem(my_dp + k, n_dp)), device_id_type=MESH)
        return c

    lax.fori_loop(1, n_sp, greet_sp, 0)
    lax.fori_loop(1, n_dp, greet_dp, 0)

    def at_sp(k):
        peer = lax.rem(me + k, n_sp)
        return peer, (peer, my_dp)

    def at_dp(k):
        peer = lax.rem(my_dp + k, n_dp)
        return peer, (me, peer)

    def gather_copy(buf, mine, where, send, recv, k):
        peer, dev = where(k)
        start = pltpu.make_async_remote_copy(
            src_ref=buf.at[mine], dst_ref=buf.at[mine], send_sem=send.at[peer],
            recv_sem=recv.at[mine], device_id=dev, device_id_type=MESH)
        wait = pltpu.make_async_remote_copy(
            src_ref=buf.at[mine], dst_ref=buf.at[peer], send_sem=send.at[peer],
            recv_sem=recv.at[peer], device_id=dev, device_id_type=MESH)
        return start, wait

    def begin(buf, mine, n, where, send, recv):
        def go(k, c):
            gather_copy(buf, mine, where, send, recv, k)[0].start()
            return c
        lax.fori_loop(1, n, go, 0)

    def finish(buf, mine, n, where, send, recv):
        def go(k, c):
            gather_copy(buf, mine, where, send, recv, k)[1].wait()
            return c
        lax.fori_loop(1, n, go, 0)

    partner = me + 1 - 2 * lax.rem(me, 2)

    def push(buf, slot, peer, send, recv):
        return pltpu.make_async_remote_copy(
            src_ref=buf.at[slot], dst_ref=buf.at[slot], send_sem=send,
            recv_sem=recv.at[slot], device_id=(peer, my_dp), device_id_type=MESH)

    def alike(k):
        return lax.rem(me + 2 * k, n_sp)

    def beside(tile):
        return tile + 1 - 2 * lax.rem(tile, 2)

    def pair_begin(buf, send, recv):
        def go(k, c):
            push(buf, me, alike(k), send.at[alike(k)], recv).start()
            return c
        lax.fori_loop(1, n_sp // 2, go, 0)
        push(buf, me, partner, send.at[partner], recv).start()

    def pair_relay(buf, send, recv):
        def go(k, c):
            tile = alike(k)
            push(buf, tile, partner, send.at[beside(tile)], recv).wait_recv()
            push(buf, tile, partner, send.at[beside(tile)], recv).start()
            return c
        lax.fori_loop(1, n_sp // 2, go, 0)

    def pair_finish(buf, send, recv):
        push(buf, partner, partner, send.at[partner], recv).wait()
        def go(k, c):
            tile = alike(k)
            push(buf, me, tile, send.at[tile], recv).wait_send()
            push(buf, beside(tile), partner, send.at[beside(tile)], recv).wait()
            return c
        lax.fori_loop(1, n_sp // 2, go, 0)

    r64 = lax.broadcasted_iota(jnp.int32, (wide, chan), 0)
    ra = lax.broadcasted_iota(jnp.int32, (wide, wide), 0)
    rb = lax.broadcasted_iota(jnp.int32, (wide, wide), 1)
    mirror = jnp.where(ra + rb == side - 1, 1.0, 0.0).astype(BF16)

    def flip(v):
        return jnp.dot(mirror, v, preferred_element_type=F32)

    s8 = lax.broadcasted_iota(jnp.int32, (ROWS, 8, chan), 1)

    def column(block, at):
        return jnp.sum(jnp.where(s8 == at, block, 0.0), axis=1)

    tail = jnp.zeros((wide - side, chan), F32)

    def widen(v):
        return jnp.concatenate([v, tail], axis=0)

    for c in range(chunks):
        lo = c * ROWS
        left = x_in[lo:lo + ROWS, 0:8, :].astype(F32)
        right = x_in[lo:lo + ROWS, side - 8:side, :].astype(F32)
        col_a[lo:lo + ROWS, :] = silu(column(left, 0))
        col_b[lo:lo + ROWS, :] = silu(column(right, 7))
        col_g[0, lo:lo + ROWS, :] = column(g_in[lo:lo + ROWS, 0:8, :].astype(F32), 0)
        col_g[1, lo:lo + ROWS, :] = column(g_in[lo:lo + ROWS, side - 8:side, :].astype(F32), 7)
    col_a[side:wide, :] = tail
    col_b[side:wide, :] = tail
    col_g[0, side:wide, :] = tail
    col_g[1, side:wide, :] = tail
    fwd[me, 0] = widen(silu(x_in[0].astype(F32))).astype(BF16)
    fwd[me, 1] = col_b[...].astype(BF16)
    fwd[me, 2] = flip(widen(silu(x_in[side - 1].astype(F32))).astype(BF16)).astype(BF16)
    fwd[me, 3] = flip(col_a[...].astype(BF16)).astype(BF16)
    for r in range(3):
        for c in range(3):
            block = w_in[2 - r, (2 - c) * chan:(3 - c) * chan, :].astype(F32)
            wt[r, c * chan:(c + 1) * chan, :] = block.T.astype(BF16)
    zero_row = jnp.zeros((wide, 3 * chan), BF16)
    for row in (0, 1, side + 2, side + 3):
        gtaps[row] = zero_row

    def spread_grad(c, carry):
        for k in range(ROWS):
            i = c * ROWS + k
            g = widen(g_in[i].astype(F32))
            gtaps[i + 2, :, 0:chan] = pltpu.roll(g, 2, 0).astype(BF16)
            gtaps[i + 2, :, chan:2 * chan] = pltpu.roll(g, 1, 0).astype(BF16)
            gtaps[i + 2, :, 2 * chan:] = g.astype(BF16)
        return carry

    lax.fori_loop(0, chunks, spread_grad, 0)

    def put_taps(row, a):
        taps[row, :, 0:chan] = pltpu.roll(a, 1, 0).astype(BF16)
        taps[row, :, chan:2 * chan] = a.astype(BF16)
        taps[row, :, 2 * chan:] = pltpu.roll(a, wide - 1, 0).astype(BF16)

    def spread_act(c, carry):
        for k in range(ROWS):
            i = c * ROWS + k
            put_taps(i + 1, widen(silu(x_in[i].astype(F32))))
        return carry

    lax.fori_loop(0, chunks, spread_act, 0)

    taps[0] = zero_row
    taps[side + 1] = zero_row
    pl.semaphore_wait(barrier, n_sp + n_dp - 2)
    pair_begin(fwd, fs, fr)

    acc[...] = jnp.zeros_like(acc)

    def kernel_chunk(c, carry):
        i0 = c * ROWS
        gt = gtaps[pl.ds(i0 + 2, ROWS), :, 2 * chan:].reshape(ROWS * wide, chan).T
        for r in range(3):
            acc[r] += jnp.dot(
                gt, taps[pl.ds(i0 + r, ROWS)].reshape(ROWS * wide, 3 * chan),
                preferred_element_type=F32)
        return carry

    lax.fori_loop(0, chunks, kernel_chunk, 0)
    def grad_rows(first, count):
        total = jnp.zeros((count * wide, chan), F32)
        for r in range(3):
            total += jnp.dot(
                gtaps[pl.ds(first + r, count)].reshape(count * wide, 3 * chan), wt[r],
                preferred_element_type=F32)
        pad_grad[pl.ds(first, count)] = total.reshape(count, wide, chan)

    def grad_chunk(c, carry):
        grad_rows(c * ROWS, ROWS)
        return carry

    lax.fori_loop(0, chunks, grad_chunk, 0)
    grad_rows(side, 2)

    pair_relay(fwd, fs, fr)

    for c in range(chunks):
        lo = c * ROWS
        col_a[lo:lo + ROWS, :] = column(pad_grad[lo + 1:lo + 1 + ROWS, 0:8, :], 0)
        col_b[lo:lo + ROWS, :] = column(pad_grad[lo + 1:lo + 1 + ROWS, side:side + 8, :], 1)
    first_row = pad_grad[0]
    last_row = pad_grad[side + 1]
    top = pltpu.roll(first_row, wide - 1, 0)
    bottom = pltpu.roll(last_row, wide - 1, 0)

    def pack(v, corner):
        return jnp.where(r64 < side, v, jnp.where(r64 == side, corner, 0.0)).astype(BF16)

    back[me, 0] = pack(top, first_row[0:1])
    back[me, 1] = pack(col_b[...], first_row[side + 1:side + 2])
    back[me, 2] = pack(flip(bottom.astype(BF16)), last_row[side + 1:side + 2])
    back[me, 3] = pack(flip(col_a[...].astype(BF16)), last_row[0:1])

    pair_finish(fwd, fs, fr)

    def near(buf, e):
        return buf[adj[0, 0, e], adj[0, 1, e]]

    def near_corner(buf, k, row):
        return buf[adj[0, 0, 4 + k], adj[0, 1, 4 + k]].astype(F32)[row:row + 1]

    corner = [near_corner(fwd, k, 0) for k in range(4)]

    def rim_row(v, behind, ahead):
        return jnp.where(r64 < side, v, jnp.where(r64 == side, behind, jnp.where(r64 == wide - 1, ahead, 0.0)))

    put_taps(0, rim_row(flip(near(fwd, 0)), corner[1], corner[0]))
    put_taps(side + 1, rim_row(near(fwd, 2).astype(F32), corner[2], corner[3]))
    col_a[...] = near(fwd, 3).astype(F32)
    col_b[...] = flip(near(fwd, 1))

    def turned(v):
        return v.astype(BF16).T

    acc[0] += jnp.dot(turned(gtaps[2, :, 2 * chan:]), taps[0], preferred_element_type=F32)
    acc[2] += jnp.dot(turned(gtaps[side + 1, :, 2 * chan:]), taps[side + 1], preferred_element_type=F32)
    for e, rim in ((0, col_a), (1, col_b)):
        gt = turned(col_g[e])
        at = 2 * e * chan
        for r, turn in ((0, 1), (1, 0), (2, wide - 1)):
            v = pltpu.roll(rim[...], turn, 0) if turn else rim[...]
            acc[r, :, at:at + chan] += jnp.dot(gt, v.astype(BF16), preferred_element_type=F32)
    for r in range(3):
        for c in range(3):
            at = (3 * r + c) * chan
            wgf[at:at + chan, :] = acc[r, :, c * chan:(c + 1) * chan].T
    size = parts.shape[1] - 16
    used = 9 * chan
    if n_sp * size > used:
        wgf[used:, :] = jnp.zeros((n_sp * size - used, chan), F32)

    def scatter_copy(k):
        peer, dev = at_sp(k)
        src = wg.at[peer]
        start = pltpu.make_async_remote_copy(
            src_ref=src, dst_ref=parts.at[me], send_sem=ss.at[peer],
            recv_sem=sr.at[me], device_id=dev, device_id_type=MESH)
        wait = pltpu.make_async_remote_copy(
            src_ref=src, dst_ref=parts.at[peer], send_sem=ss.at[peer],
            recv_sem=sr.at[peer], device_id=dev, device_id_type=MESH)
        return start, wait

    def own_rows(peer):
        return wgf[pl.ds(pl.multiple_of(peer * size, 16), size), :]

    def scatter_start(k, c):
        peer = lax.rem(me + k, n_sp)
        wg[peer] = encode(own_rows(peer))
        scatter_copy(k)[0].start()
        return c

    def scatter_wait(k, c):
        scatter_copy(k)[1].wait()
        return c

    lax.fori_loop(1, n_sp, scatter_start, 0)
    parts[me] = encode(own_rows(me))
    pair_begin(back, bs, br)

    s16 = lax.broadcasted_iota(jnp.int32, (ROWS, 16, chan), 1)
    at_right = (side - 1) // 16 * 16
    for c in range(chunks):
        lo = c * ROWS
        v = taps[lo + 1:lo + 1 + ROWS, 0:16, 0:chan].astype(F32)
        v = jnp.where(s16 == 0, col_a[lo:lo + ROWS, :][:, None, :], v)
        taps[lo + 1:lo + 1 + ROWS, 0:16, 0:chan] = v.astype(BF16)
        v = taps[lo + 1:lo + 1 + ROWS, at_right:at_right + 16, 2 * chan:].astype(F32)
        v = jnp.where(s16 == side - 1 - at_right, col_b[lo:lo + ROWS, :][:, None, :], v)
        taps[lo + 1:lo + 1 + ROWS, at_right:at_right + 16, 2 * chan:] = v.astype(BF16)


    def conv_chunk(c, carry):
        i0 = c * ROWS
        total = jnp.zeros((ROWS * wide, chan), F32)
        for r in range(3):
            total += jnp.dot(
                taps[pl.ds(i0 + r, ROWS)].reshape(ROWS * wide, 3 * chan), w_in[r],
                preferred_element_type=F32)
        conv = total.reshape(ROWS, wide, chan)[:, :side, :]
        field = x_in[pl.ds(i0, ROWS)].astype(F32)
        out[pl.ds(i0, ROWS)] = (field + conv + bias[...].reshape(1, 1, chan)).astype(BF16)
        return carry

    lax.fori_loop(0, chunks, conv_chunk, 0)
    out_copy = pltpu.make_async_copy(out, out_hbm, lo_sem.at[0])
    out_copy.start()

    lax.fori_loop(1, n_sp, scatter_wait, 0)
    mine = lax.fori_loop(0, n_sp, lambda k, t: t + decode(parts[k]), jnp.zeros((size, chan), F32))
    dps[my_dp] = encode(mine)
    begin(dps, my_dp, n_dp, at_dp, ds_, dr)
    pair_relay(back, bs, br)

    finish(dps, my_dp, n_dp, at_dp, ds_, dr)
    total = decode(dps[0])
    for d in range(1, n_dp):
        total = total + decode(dps[d])
    full[me] = encode(total)
    begin(full, me, n_sp, at_sp, gs, gr)

    pair_finish(back, bs, br)

    def inner(v):
        return jnp.where(r64 < side, v, 0.0)

    ends = [near_corner(back, k, side) for k in range(4)]
    pad_grad[1] += pltpu.roll(inner(flip(near(back, 0))), 1, 0)
    pad_grad[side] += pltpu.roll(inner(near(back, 2).astype(F32)), 1, 0)
    col_a[...] = inner(near(back, 3).astype(F32)) + jnp.where(r64 == 0, ends[0], jnp.where(r64 == side - 1, ends[3], 0.0))
    col_b[...] = inner(flip(near(back, 1))) + jnp.where(r64 == 0, ends[1], jnp.where(r64 == side - 1, ends[2], 0.0))

    r56 = lax.broadcasted_iota(jnp.int32, (side, chan), 0)

    def finish_rows(c, carry):
        for k in range(ROWS):
            i = c * ROWS + k
            p = pltpu.roll(pad_grad[i + 1], wide - 1, 0)[:side]
            p = p + jnp.where(r56 == 0, col_a[pl.ds(i, 1), :], jnp.where(r56 == side - 1, col_b[pl.ds(i, 1), :], 0.0))
            v = x_in[i].astype(F32)
            s = 1.0 / (1.0 + jnp.exp(-v))
            gin_out[i] = (g_in[i].astype(F32) + p * s * (1.0 + v * (1.0 - s))).astype(BF16)
        return carry

    lax.fori_loop(0, chunks, finish_rows, 0)
    gin_copy = pltpu.make_async_copy(gin_out, gin_hbm, lo_sem.at[1])
    gin_copy.start()

    finish(full, me, n_sp, at_sp, gs, gr)
    def open_rows(k, c):
        wgf[pl.ds(pl.multiple_of(k * size, 16), size), :] = decode(full[k])
        return c

    lax.fori_loop(0, n_sp, open_rows, 0)
    kernel_copy = pltpu.make_async_copy(wgf.at[pl.ds(0, used)], wg_out, lo_sem.at[2])
    kernel_copy.start()
    kernel_copy.wait()
    gin_copy.wait()
    out_copy.wait()


def hand_on(a_in, b_in, c_in, a_out, b_out, c_out, a, b, c, sems):
    loads = [pltpu.make_async_copy(src, mid, sems.at[k]) for k, (src, mid) in enumerate(((a_in, a), (b_in, b), (c_in, c)))]
    stores = [pltpu.make_async_copy(mid, dst, sems.at[3 + k]) for k, (mid, dst) in enumerate(((a, a_out), (b, b_out), (c, c_out)))]
    for one in loads:
        one.start()
    for load, store in zip(loads, stores):
        load.wait()
        store.start()
    for one in stores:
        one.wait()


def per_device(n_sp, n_dp, block_in, weights, out_bias, adjacency, cotangent):
    side, chan = block_in.shape[2], block_in.shape[4]
    wide = wide_of(side)
    size = -(-9 * chan // (16 * n_sp)) * 16
    vmem = pl.BlockSpec(memory_space=pltpu.VMEM)
    hbm = pl.BlockSpec(memory_space=pl.ANY)
    sem = pltpu.SemaphoreType.DMA
    shapes = (
        jax.ShapeDtypeStruct((side, side, chan), BF16),
        jax.ShapeDtypeStruct((9 * chan, chan), F32),
        jax.ShapeDtypeStruct((side, side, chan), BF16),
    )
    held = pl.pallas_call(
        functools.partial(block_kernel, n_sp, n_dp, side),
        out_shape=shapes,
        in_specs=[pl.BlockSpec(memory_space=pltpu.SMEM), vmem, vmem, vmem, vmem],
        out_specs=(hbm, hbm, hbm),
        scratch_shapes=[
            pltpu.VMEM((side + 2, wide, 3 * chan), BF16),
            pltpu.VMEM((side + 4, wide, 3 * chan), BF16),
            pltpu.VMEM((side + 2, wide, chan), F32),
            pltpu.VMEM((3, 3 * chan, chan), BF16),
            pltpu.VMEM((3, chan, 3 * chan), F32),
            pltpu.VMEM((wide, chan), F32),
            pltpu.VMEM((wide, chan), F32),
            pltpu.VMEM((n_sp, 4, wide, chan), BF16),
            pltpu.VMEM((n_sp, 4, wide, chan), BF16),
            pltpu.VMEM((n_sp, size + 16, chan), jnp.int16),
            pltpu.VMEM((n_sp, size + 16, chan), jnp.int16),
            pltpu.VMEM((n_dp, size + 16, chan), jnp.int16),
            pltpu.VMEM((n_sp, size + 16, chan), jnp.int16),
            sem((n_sp,)), sem((n_sp,)), sem((n_sp,)), sem((n_sp,)), sem((n_sp,)), sem((n_sp,)),
            sem((n_dp,)), sem((n_dp,)), sem((n_sp,)), sem((n_sp,)),
            pltpu.VMEM((side, side, chan), BF16),
            pltpu.VMEM((side, side, chan), BF16),
            pltpu.VMEM((n_sp * size, chan), F32),
            sem((3,)),
            pltpu.VMEM((2, wide, chan), F32),
        ],
        compiler_params=pltpu.CompilerParams(
            collective_id=0, has_side_effects=True, vmem_limit_bytes=56 * 2**20),
    )(
        adjacency.transpose(0, 2, 1), block_in[0, 0], weights.reshape(3, 3 * chan, chan), out_bias.reshape(1, chan),
        cotangent[0, 0],
    )
    result, wgrad, grad_in = pl.pallas_call(
        hand_on,
        out_shape=shapes,
        in_specs=[hbm, hbm, hbm],
        out_specs=(hbm, hbm, hbm),
        scratch_shapes=[pltpu.VMEM(one.shape, one.dtype) for one in shapes] + [sem((6,))],
    )(*held)
    return (result[None, None], wgrad.reshape(weights.shape), grad_in[None, None])


def solution(mesh):
    placed = (
        P("dp", "space", None, None, None),
        P(),
        P(),
        P("space", None, None),
        P("dp", "space", None, None, None),
    )
    return jax.shard_map(
        functools.partial(per_device, mesh.shape["space"], mesh.shape["dp"]),
        mesh=mesh,
        in_specs=placed,
        out_specs=(P("dp", "space", None, None, None), P(), P("dp", "space", None, None, None)),
        check_vma=False,
    )
```

```python
import functools

import jax
import jax.numpy as jnp
from jax import lax
from jax.experimental import pallas as pl
from jax.experimental.pallas import tpu as pltpu
from jax.sharding import PartitionSpec as P

MESH = pl.DeviceIdType.MESH
ROWS = 8
F32 = jnp.float32
BF16 = jnp.bfloat16


def silu(v):
    return v / (1.0 + jnp.exp(-v))


def encode(v):
    top = jnp.maximum(jnp.max(jnp.abs(v), axis=0, keepdims=True), 1e-30)
    power = jnp.ceil(jnp.log2(top))
    code = jnp.clip(jnp.round(v * jnp.exp2(15.0 - power)), -32767.0, 32767.0)
    rows = jnp.concatenate([code, jnp.broadcast_to(power, (16, v.shape[1]))], axis=0)
    return rows.astype(jnp.int32).astype(jnp.int16)


def decode(rows):
    v = rows.astype(jnp.int32).astype(F32)
    size = v.shape[0] - 16
    return v[:size] * jnp.exp2(v[size:size + 1] - 15.0)


def wide_of(side):
    return -(-(side + 4) // 16) * 16


def block_kernel(
    n_sp, n_dp, side,
    adj, x_in, w_in, bias, g_in,
    out_hbm, wg_out, gin_hbm,
    taps, gtaps, pad_grad, wt, acc, col_a, col_b, fwd, back, wg, parts, dps, full,
    fs, fr, bs, br, ss, sr, ds_, dr, gs, gr, out, gin_out, wgf, lo_sem, col_g,
):
    wide = wide_of(side)
    chan = 128
    chunks = side // ROWS
    me = lax.axis_index("space")
    my_dp = lax.axis_index("dp")

    barrier = pltpu.get_barrier_semaphore()

    def greet_sp(k, c):
        pl.semaphore_signal(barrier, inc=1, device_id=(lax.rem(me + k, n_sp), my_dp), device_id_type=MESH)
        return c

    def greet_dp(k, c):
        pl.semaphore_signal(barrier, inc=1, device_id=(me, lax.rem(my_dp + k, n_dp)), device_id_type=MESH)
        return c

    lax.fori_loop(1, n_sp, greet_sp, 0)
    lax.fori_loop(1, n_dp, greet_dp, 0)

    def at_sp(k):
        peer = lax.rem(me + k, n_sp)
        return peer, (peer, my_dp)

    def at_dp(k):
        peer = lax.rem(my_dp + k, n_dp)
        return peer, (me, peer)

    def gather_copy(buf, mine, where, send, recv, k):
        peer, dev = where(k)
        start = pltpu.make_async_remote_copy(
            src_ref=buf.at[mine], dst_ref=buf.at[mine], send_sem=send.at[peer],
            recv_sem=recv.at[mine], device_id=dev, device_id_type=MESH)
        wait = pltpu.make_async_remote_copy(
            src_ref=buf.at[mine], dst_ref=buf.at[peer], send_sem=send.at[peer],
            recv_sem=recv.at[peer], device_id=dev, device_id_type=MESH)
        return start, wait

    def begin(buf, mine, n, where, send, recv):
        def go(k, c):
            gather_copy(buf, mine, where, send, recv, k)[0].start()
            return c
        lax.fori_loop(1, n, go, 0)

    def finish(buf, mine, n, where, send, recv):
        def go(k, c):
            gather_copy(buf, mine, where, send, recv, k)[1].wait()
            return c
        lax.fori_loop(1, n, go, 0)

    partner = me + 1 - 2 * lax.rem(me, 2)

    def push(buf, slot, peer, send, recv):
        return pltpu.make_async_remote_copy(
            src_ref=buf.at[slot], dst_ref=buf.at[slot], send_sem=send,
            recv_sem=recv.at[slot], device_id=(peer, my_dp), device_id_type=MESH)

    def alike(k):
        return lax.rem(me + 2 * k, n_sp)

    def beside(tile):
        return tile + 1 - 2 * lax.rem(tile, 2)

    def pair_begin(buf, send, recv):
        def go(k, c):
            push(buf, me, alike(k), send.at[alike(k)], recv).start()
            return c
        lax.fori_loop(1, n_sp // 2, go, 0)
        push(buf, me, partner, send.at[partner], recv).start()

    def pair_relay(buf, send, recv):
        def go(k, c):
            tile = alike(k)
            push(buf, tile, partner, send.at[beside(tile)], recv).wait_recv()
            push(buf, tile, partner, send.at[beside(tile)], recv).start()
            return c
        lax.fori_loop(1, n_sp // 2, go, 0)

    def pair_finish(buf, send, recv):
        push(buf, partner, partner, send.at[partner], recv).wait()
        def go(k, c):
            tile = alike(k)
            push(buf, me, tile, send.at[tile], recv).wait_send()
            push(buf, beside(tile), partner, send.at[beside(tile)], recv).wait()
            return c
        lax.fori_loop(1, n_sp // 2, go, 0)

    r64 = lax.broadcasted_iota(jnp.int32, (wide, chan), 0)
    ra = lax.broadcasted_iota(jnp.int32, (wide, wide), 0)
    rb = lax.broadcasted_iota(jnp.int32, (wide, wide), 1)
    mirror = jnp.where(ra + rb == side - 1, 1.0, 0.0).astype(BF16)

    def flip(v):
        return jnp.dot(mirror, v, preferred_element_type=F32)

    s8 = lax.broadcasted_iota(jnp.int32, (ROWS, 8, chan), 1)

    def column(block, at):
        return jnp.sum(jnp.where(s8 == at, block, 0.0), axis=1)

    tail = jnp.zeros((wide - side, chan), F32)

    def widen(v):
        return jnp.concatenate([v, tail], axis=0)

    for c in range(chunks):
        lo = c * ROWS
        left = x_in[lo:lo + ROWS, 0:8, :].astype(F32)
        right = x_in[lo:lo + ROWS, side - 8:side, :].astype(F32)
        col_a[lo:lo + ROWS, :] = silu(column(left, 0))
        col_b[lo:lo + ROWS, :] = silu(column(right, 7))
        col_g[0, lo:lo + ROWS, :] = column(g_in[lo:lo + ROWS, 0:8, :].astype(F32), 0)
        col_g[1, lo:lo + ROWS, :] = column(g_in[lo:lo + ROWS, side - 8:side, :].astype(F32), 7)
    col_a[side:wide, :] = tail
    col_b[side:wide, :] = tail
    col_g[0, side:wide, :] = tail
    col_g[1, side:wide, :] = tail
    fwd[me, 0] = widen(silu(x_in[0].astype(F32))).astype(BF16)
    fwd[me, 1] = col_b[...].astype(BF16)
    fwd[me, 2] = flip(widen(silu(x_in[side - 1].astype(F32))).astype(BF16)).astype(BF16)
    fwd[me, 3] = flip(col_a[...].astype(BF16)).astype(BF16)
    for r in range(3):
        for c in range(3):
            block = w_in[2 - r, (2 - c) * chan:(3 - c) * chan, :].astype(F32)
            wt[r, c * chan:(c + 1) * chan, :] = block.T.astype(BF16)
    zero_row = jnp.zeros((wide, 3 * chan), BF16)
    for row in (0, 1, side + 2, side + 3):
        gtaps[row] = zero_row

    def spread_grad(c, carry):
        for k in range(ROWS):
            i = c * ROWS + k
            g = widen(g_in[i].astype(F32))
            gtaps[i + 2, :, 0:chan] = pltpu.roll(g, 2, 0).astype(BF16)
            gtaps[i + 2, :, chan:2 * chan] = pltpu.roll(g, 1, 0).astype(BF16)
            gtaps[i + 2, :, 2 * chan:] = g.astype(BF16)
        return carry

    lax.fori_loop(0, chunks, spread_grad, 0)

    def put_taps(row, a):
        taps[row, :, 0:chan] = pltpu.roll(a, 1, 0).astype(BF16)
        taps[row, :, chan:2 * chan] = a.astype(BF16)
        taps[row, :, 2 * chan:] = pltpu.roll(a, wide - 1, 0).astype(BF16)

    def spread_act(c, carry):
        for k in range(ROWS):
            i = c * ROWS + k
            put_taps(i + 1, widen(silu(x_in[i].astype(F32))))
        return carry

    lax.fori_loop(0, chunks, spread_act, 0)

    taps[0] = zero_row
    taps[side + 1] = zero_row
    pl.semaphore_wait(barrier, n_sp + n_dp - 2)
    pair_begin(fwd, fs, fr)

    acc[...] = jnp.zeros_like(acc)

    def kernel_chunk(c, carry):
        i0 = c * ROWS
        gt = gtaps[pl.ds(i0 + 2, ROWS), :, 2 * chan:].reshape(ROWS * wide, chan).T
        for r in range(3):
            acc[r] += jnp.dot(
                gt, taps[pl.ds(i0 + r, ROWS)].reshape(ROWS * wide, 3 * chan),
                preferred_element_type=F32)
        return carry

    lax.fori_loop(0, chunks, kernel_chunk, 0)
    pair_relay(fwd, fs, fr)
    pair_finish(fwd, fs, fr)

    def near(buf, e):
        return buf[adj[0, 0, e], adj[0, 1, e]]

    def near_corner(buf, k, row):
        return buf[adj[0, 0, 4 + k], adj[0, 1, 4 + k]].astype(F32)[row:row + 1]

    corner = [near_corner(fwd, k, 0) for k in range(4)]

    def rim_row(v, behind, ahead):
        return jnp.where(r64 < side, v, jnp.where(r64 == side, behind, jnp.where(r64 == wide - 1, ahead, 0.0)))

    put_taps(0, rim_row(flip(near(fwd, 0)), corner[1], corner[0]))
    put_taps(side + 1, rim_row(near(fwd, 2).astype(F32), corner[2], corner[3]))
    col_a[...] = near(fwd, 3).astype(F32)
    col_b[...] = flip(near(fwd, 1))

    def turned(v):
        return v.astype(BF16).T

    acc[0] += jnp.dot(turned(gtaps[2, :, 2 * chan:]), taps[0], preferred_element_type=F32)
    acc[2] += jnp.dot(turned(gtaps[side + 1, :, 2 * chan:]), taps[side + 1], preferred_element_type=F32)
    for e, rim in ((0, col_a), (1, col_b)):
        gt = turned(col_g[e])
        at = 2 * e * chan
        for r, turn in ((0, 1), (1, 0), (2, wide - 1)):
            v = pltpu.roll(rim[...], turn, 0) if turn else rim[...]
            acc[r, :, at:at + chan] += jnp.dot(gt, v.astype(BF16), preferred_element_type=F32)
    for r in range(3):
        for c in range(3):
            at = (3 * r + c) * chan
            wgf[at:at + chan, :] = acc[r, :, c * chan:(c + 1) * chan].T
    size = parts.shape[1] - 16
    used = 9 * chan
    if n_sp * size > used:
        wgf[used:, :] = jnp.zeros((n_sp * size - used, chan), F32)

    def scatter_copy(k):
        peer, dev = at_sp(k)
        src = wg.at[peer]
        start = pltpu.make_async_remote_copy(
            src_ref=src, dst_ref=parts.at[me], send_sem=ss.at[peer],
            recv_sem=sr.at[me], device_id=dev, device_id_type=MESH)
        wait = pltpu.make_async_remote_copy(
            src_ref=src, dst_ref=parts.at[peer], send_sem=ss.at[peer],
            recv_sem=sr.at[peer], device_id=dev, device_id_type=MESH)
        return start, wait

    def own_rows(peer):
        return wgf[pl.ds(pl.multiple_of(peer * size, 16), size), :]

    def scatter_start(k, c):
        peer = lax.rem(me + k, n_sp)
        wg[peer] = encode(own_rows(peer))
        scatter_copy(k)[0].start()
        return c

    def scatter_wait(k, c):
        scatter_copy(k)[1].wait()
        return c

    lax.fori_loop(1, n_sp, scatter_start, 0)
    parts[me] = encode(own_rows(me))

    s16 = lax.broadcasted_iota(jnp.int32, (ROWS, 16, chan), 1)
    at_right = (side - 1) // 16 * 16
    for c in range(chunks):
        lo = c * ROWS
        v = taps[lo + 1:lo + 1 + ROWS, 0:16, 0:chan].astype(F32)
        v = jnp.where(s16 == 0, col_a[lo:lo + ROWS, :][:, None, :], v)
        taps[lo + 1:lo + 1 + ROWS, 0:16, 0:chan] = v.astype(BF16)
        v = taps[lo + 1:lo + 1 + ROWS, at_right:at_right + 16, 2 * chan:].astype(F32)
        v = jnp.where(s16 == side - 1 - at_right, col_b[lo:lo + ROWS, :][:, None, :], v)
        taps[lo + 1:lo + 1 + ROWS, at_right:at_right + 16, 2 * chan:] = v.astype(BF16)


    def grad_rows(first, count):
        total = jnp.zeros((count * wide, chan), F32)
        for r in range(3):
            total += jnp.dot(
                gtaps[pl.ds(first + r, count)].reshape(count * wide, 3 * chan), wt[r],
                preferred_element_type=F32)
        pad_grad[pl.ds(first, count)] = total.reshape(count, wide, chan)

    def grad_chunk(c, carry):
        grad_rows(c * ROWS, ROWS)
        return carry

    lax.fori_loop(0, chunks, grad_chunk, 0)
    grad_rows(side, 2)

    for c in range(chunks):
        lo = c * ROWS
        col_a[lo:lo + ROWS, :] = column(pad_grad[lo + 1:lo + 1 + ROWS, 0:8, :], 0)
        col_b[lo:lo + ROWS, :] = column(pad_grad[lo + 1:lo + 1 + ROWS, side:side + 8, :], 1)
    first_row = pad_grad[0]
    last_row = pad_grad[side + 1]
    top = pltpu.roll(first_row, wide - 1, 0)
    bottom = pltpu.roll(last_row, wide - 1, 0)

    def pack(v, corner):
        return jnp.where(r64 < side, v, jnp.where(r64 == side, corner, 0.0)).astype(BF16)

    back[me, 0] = pack(top, first_row[0:1])
    back[me, 1] = pack(col_b[...], first_row[side + 1:side + 2])
    back[me, 2] = pack(flip(bottom.astype(BF16)), last_row[side + 1:side + 2])
    back[me, 3] = pack(flip(col_a[...].astype(BF16)), last_row[0:1])

    pair_begin(back, bs, br)

    lax.fori_loop(1, n_sp, scatter_wait, 0)
    mine = lax.fori_loop(0, n_sp, lambda k, t: t + decode(parts[k]), jnp.zeros((size, chan), F32))
    dps[my_dp] = encode(mine)
    begin(dps, my_dp, n_dp, at_dp, ds_, dr)

    def conv_chunk(c, carry):
        i0 = c * ROWS
        total = jnp.zeros((ROWS * wide, chan), F32)
        for r in range(3):
            total += jnp.dot(
                taps[pl.ds(i0 + r, ROWS)].reshape(ROWS * wide, 3 * chan), w_in[r],
                preferred_element_type=F32)
        conv = total.reshape(ROWS, wide, chan)[:, :side, :]
        field = x_in[pl.ds(i0, ROWS)].astype(F32)
        out[pl.ds(i0, ROWS)] = (field + conv + bias[...].reshape(1, 1, chan)).astype(BF16)
        return carry

    lax.fori_loop(0, chunks, conv_chunk, 0)
    out_copy = pltpu.make_async_copy(out, out_hbm, lo_sem.at[0])
    out_copy.start()

    pair_relay(back, bs, br)

    finish(dps, my_dp, n_dp, at_dp, ds_, dr)
    total = decode(dps[0])
    for d in range(1, n_dp):
        total = total + decode(dps[d])
    full[me] = encode(total)
    begin(full, me, n_sp, at_sp, gs, gr)

    pair_finish(back, bs, br)

    def inner(v):
        return jnp.where(r64 < side, v, 0.0)

    ends = [near_corner(back, k, side) for k in range(4)]
    pad_grad[1] += pltpu.roll(inner(flip(near(back, 0))), 1, 0)
    pad_grad[side] += pltpu.roll(inner(near(back, 2).astype(F32)), 1, 0)
    col_a[...] = inner(near(back, 3).astype(F32)) + jnp.where(r64 == 0, ends[0], jnp.where(r64 == side - 1, ends[3], 0.0))
    col_b[...] = inner(flip(near(back, 1))) + jnp.where(r64 == 0, ends[1], jnp.where(r64 == side - 1, ends[2], 0.0))

    r56 = lax.broadcasted_iota(jnp.int32, (side, chan), 0)

    def finish_rows(c, carry):
        for k in range(ROWS):
            i = c * ROWS + k
            p = pltpu.roll(pad_grad[i + 1], wide - 1, 0)[:side]
            p = p + jnp.where(r56 == 0, col_a[pl.ds(i, 1), :], jnp.where(r56 == side - 1, col_b[pl.ds(i, 1), :], 0.0))
            v = x_in[i].astype(F32)
            s = 1.0 / (1.0 + jnp.exp(-v))
            gin_out[i] = (g_in[i].astype(F32) + p * s * (1.0 + v * (1.0 - s))).astype(BF16)
        return carry

    lax.fori_loop(0, chunks, finish_rows, 0)
    gin_copy = pltpu.make_async_copy(gin_out, gin_hbm, lo_sem.at[1])
    gin_copy.start()

    finish(full, me, n_sp, at_sp, gs, gr)
    def open_rows(k, c):
        wgf[pl.ds(pl.multiple_of(k * size, 16), size), :] = decode(full[k])
        return c

    lax.fori_loop(0, n_sp, open_rows, 0)
    kernel_copy = pltpu.make_async_copy(wgf.at[pl.ds(0, used)], wg_out, lo_sem.at[2])
    kernel_copy.start()
    kernel_copy.wait()
    gin_copy.wait()
    out_copy.wait()


def hand_on(a_in, b_in, c_in, a_out, b_out, c_out, a, b, c, sems):
    loads = [pltpu.make_async_copy(src, mid, sems.at[k]) for k, (src, mid) in enumerate(((a_in, a), (b_in, b), (c_in, c)))]
    stores = [pltpu.make_async_copy(mid, dst, sems.at[3 + k]) for k, (mid, dst) in enumerate(((a, a_out), (b, b_out), (c, c_out)))]
    for one in loads:
        one.start()
    for load, store in zip(loads, stores):
        load.wait()
        store.start()
    for one in stores:
        one.wait()


def per_device(n_sp, n_dp, block_in, weights, out_bias, adjacency, cotangent):
    side, chan = block_in.shape[2], block_in.shape[4]
    wide = wide_of(side)
    size = -(-9 * chan // (16 * n_sp)) * 16
    vmem = pl.BlockSpec(memory_space=pltpu.VMEM)
    hbm = pl.BlockSpec(memory_space=pl.ANY)
    sem = pltpu.SemaphoreType.DMA
    shapes = (
        jax.ShapeDtypeStruct((side, side, chan), BF16),
        jax.ShapeDtypeStruct((9 * chan, chan), F32),
        jax.ShapeDtypeStruct((side, side, chan), BF16),
    )
    held = pl.pallas_call(
        functools.partial(block_kernel, n_sp, n_dp, side),
        out_shape=shapes,
        in_specs=[pl.BlockSpec(memory_space=pltpu.SMEM), vmem, vmem, vmem, vmem],
        out_specs=(hbm, hbm, hbm),
        scratch_shapes=[
            pltpu.VMEM((side + 2, wide, 3 * chan), BF16),
            pltpu.VMEM((side + 4, wide, 3 * chan), BF16),
            pltpu.VMEM((side + 2, wide, chan), F32),
            pltpu.VMEM((3, 3 * chan, chan), BF16),
            pltpu.VMEM((3, chan, 3 * chan), F32),
            pltpu.VMEM((wide, chan), F32),
            pltpu.VMEM((wide, chan), F32),
            pltpu.VMEM((n_sp, 4, wide, chan), BF16),
            pltpu.VMEM((n_sp, 4, wide, chan), BF16),
            pltpu.VMEM((n_sp, size + 16, chan), jnp.int16),
            pltpu.VMEM((n_sp, size + 16, chan), jnp.int16),
            pltpu.VMEM((n_dp, size + 16, chan), jnp.int16),
            pltpu.VMEM((n_sp, size + 16, chan), jnp.int16),
            sem((n_sp,)), sem((n_sp,)), sem((n_sp,)), sem((n_sp,)), sem((n_sp,)), sem((n_sp,)),
            sem((n_dp,)), sem((n_dp,)), sem((n_sp,)), sem((n_sp,)),
            pltpu.VMEM((side, side, chan), BF16),
            pltpu.VMEM((side, side, chan), BF16),
            pltpu.VMEM((n_sp * size, chan), F32),
            sem((3,)),
            pltpu.VMEM((2, wide, chan), F32),
        ],
        compiler_params=pltpu.CompilerParams(
            collective_id=0, has_side_effects=True, vmem_limit_bytes=56 * 2**20),
    )(
        adjacency.transpose(0, 2, 1), block_in[0, 0], weights.reshape(3, 3 * chan, chan), out_bias.reshape(1, chan),
        cotangent[0, 0],
    )
    result, wgrad, grad_in = pl.pallas_call(
        hand_on,
        out_shape=shapes,
        in_specs=[hbm, hbm, hbm],
        out_specs=(hbm, hbm, hbm),
        scratch_shapes=[pltpu.VMEM(one.shape, one.dtype) for one in shapes] + [sem((6,))],
    )(*held)
    return (result[None, None], wgrad.reshape(weights.shape), grad_in[None, None])


def solution(mesh):
    placed = (
        P("dp", "space", None, None, None),
        P(),
        P(),
        P("space", None, None),
        P("dp", "space", None, None, None),
    )
    return jax.shard_map(
        functools.partial(per_device, mesh.shape["space"], mesh.shape["dp"]),
        mesh=mesh,
        in_specs=placed,
        out_specs=(P("dp", "space", None, None, None), P(), P("dp", "space", None, None, None)),
        check_vma=False,
    )
```

```python
import functools

import jax
import jax.numpy as jnp
from jax import lax
from jax.experimental import pallas as pl
from jax.experimental.pallas import tpu as pltpu
from jax.sharding import PartitionSpec as P

MESH = pl.DeviceIdType.MESH
ROWS = 8
F32 = jnp.float32
BF16 = jnp.bfloat16


def silu(v):
    return v / (1.0 + jnp.exp(-v))


def encode(v):
    top = jnp.maximum(jnp.max(jnp.abs(v), axis=0, keepdims=True), 1e-30)
    power = jnp.ceil(jnp.log2(top))
    code = jnp.clip(jnp.round(v * jnp.exp2(15.0 - power)), -32767.0, 32767.0)
    rows = jnp.concatenate([code, jnp.broadcast_to(power, (16, v.shape[1]))], axis=0)
    return rows.astype(jnp.int32).astype(jnp.int16)


def decode(rows):
    v = rows.astype(jnp.int32).astype(F32)
    size = v.shape[0] - 16
    return v[:size] * jnp.exp2(v[size:size + 1] - 15.0)


def wide_of(side):
    return -(-(side + 4) // 16) * 16


def block_kernel(
    n_sp, n_dp, side,
    adj, x_in, w_in, bias, g_in,
    out_hbm, wg_out, gin_hbm,
    taps, gtaps, pad_grad, wt, acc, col_a, col_b, fwd, back, wg, parts, dps, full,
    fs, fr, bs, br, ss, sr, ds_, dr, gs, gr, out, gin_out, wgf, lo_sem, col_g,
):
    wide = wide_of(side)
    chan = 128
    chunks = side // ROWS
    me = lax.axis_index("space")
    my_dp = lax.axis_index("dp")

    barrier = pltpu.get_barrier_semaphore()

    def greet_sp(k, c):
        pl.semaphore_signal(barrier, inc=1, device_id=(lax.rem(me + k, n_sp), my_dp), device_id_type=MESH)
        return c

    def greet_dp(k, c):
        pl.semaphore_signal(barrier, inc=1, device_id=(me, lax.rem(my_dp + k, n_dp)), device_id_type=MESH)
        return c

    lax.fori_loop(1, n_sp, greet_sp, 0)
    lax.fori_loop(1, n_dp, greet_dp, 0)

    def at_sp(k):
        peer = lax.rem(me + k, n_sp)
        return peer, (peer, my_dp)

    def at_dp(k):
        peer = lax.rem(my_dp + k, n_dp)
        return peer, (me, peer)

    def gather_copy(buf, mine, where, send, recv, k):
        peer, dev = where(k)
        start = pltpu.make_async_remote_copy(
            src_ref=buf.at[mine], dst_ref=buf.at[mine], send_sem=send.at[peer],
            recv_sem=recv.at[mine], device_id=dev, device_id_type=MESH)
        wait = pltpu.make_async_remote_copy(
            src_ref=buf.at[mine], dst_ref=buf.at[peer], send_sem=send.at[peer],
            recv_sem=recv.at[peer], device_id=dev, device_id_type=MESH)
        return start, wait

    def begin(buf, mine, n, where, send, recv):
        def go(k, c):
            gather_copy(buf, mine, where, send, recv, k)[0].start()
            return c
        lax.fori_loop(1, n, go, 0)

    def finish(buf, mine, n, where, send, recv):
        def go(k, c):
            gather_copy(buf, mine, where, send, recv, k)[1].wait()
            return c
        lax.fori_loop(1, n, go, 0)

    partner = me + 1 - 2 * lax.rem(me, 2)

    def push(buf, slot, peer, send, recv):
        return pltpu.make_async_remote_copy(
            src_ref=buf.at[slot], dst_ref=buf.at[slot], send_sem=send,
            recv_sem=recv.at[slot], device_id=(peer, my_dp), device_id_type=MESH)

    def alike(k):
        return lax.rem(me + 2 * k, n_sp)

    def beside(tile):
        return tile + 1 - 2 * lax.rem(tile, 2)

    def pair_begin(buf, send, recv):
        def go(k, c):
            push(buf, me, alike(k), send.at[alike(k)], recv).start()
            return c
        lax.fori_loop(1, n_sp // 2, go, 0)
        push(buf, me, partner, send.at[partner], recv).start()

    def pair_relay(buf, send, recv):
        def go(k, c):
            tile = alike(k)
            push(buf, tile, partner, send.at[beside(tile)], recv).wait_recv()
            push(buf, tile, partner, send.at[beside(tile)], recv).start()
            return c
        lax.fori_loop(1, n_sp // 2, go, 0)

    def pair_finish(buf, send, recv):
        push(buf, partner, partner, send.at[partner], recv).wait()
        def go(k, c):
            tile = alike(k)
            push(buf, me, tile, send.at[tile], recv).wait_send()
            push(buf, beside(tile), partner, send.at[beside(tile)], recv).wait()
            return c
        lax.fori_loop(1, n_sp // 2, go, 0)

    r64 = lax.broadcasted_iota(jnp.int32, (wide, chan), 0)
    ra = lax.broadcasted_iota(jnp.int32, (wide, wide), 0)
    rb = lax.broadcasted_iota(jnp.int32, (wide, wide), 1)
    mirror = jnp.where(ra + rb == side - 1, 1.0, 0.0).astype(BF16)

    def flip(v):
        return jnp.dot(mirror, v, preferred_element_type=F32)

    s8 = lax.broadcasted_iota(jnp.int32, (ROWS, 8, chan), 1)

    def column(block, at):
        return jnp.sum(jnp.where(s8 == at, block, 0.0), axis=1)

    tail = jnp.zeros((wide - side, chan), F32)

    def widen(v):
        return jnp.concatenate([v, tail], axis=0)

    for c in range(chunks):
        lo = c * ROWS
        left = x_in[lo:lo + ROWS, 0:8, :].astype(F32)
        right = x_in[lo:lo + ROWS, side - 8:side, :].astype(F32)
        col_a[lo:lo + ROWS, :] = silu(column(left, 0))
        col_b[lo:lo + ROWS, :] = silu(column(right, 7))
        col_g[0, lo:lo + ROWS, :] = column(g_in[lo:lo + ROWS, 0:8, :].astype(F32), 0)
        col_g[1, lo:lo + ROWS, :] = column(g_in[lo:lo + ROWS, side - 8:side, :].astype(F32), 7)
    col_a[side:wide, :] = tail
    col_b[side:wide, :] = tail
    col_g[0, side:wide, :] = tail
    col_g[1, side:wide, :] = tail
    fwd[me, 0] = widen(silu(x_in[0].astype(F32))).astype(BF16)
    fwd[me, 1] = col_b[...].astype(BF16)
    fwd[me, 2] = flip(widen(silu(x_in[side - 1].astype(F32))).astype(BF16)).astype(BF16)
    fwd[me, 3] = flip(col_a[...].astype(BF16)).astype(BF16)
    for r in range(3):
        for c in range(3):
            block = w_in[2 - r, (2 - c) * chan:(3 - c) * chan, :].astype(F32)
            wt[r, c * chan:(c + 1) * chan, :] = block.T.astype(BF16)
    zero_row = jnp.zeros((wide, 3 * chan), BF16)
    for row in (0, 1, side + 2, side + 3):
        gtaps[row] = zero_row

    def spread_grad(c, carry):
        for k in range(ROWS):
            i = c * ROWS + k
            g = widen(g_in[i].astype(F32))
            gtaps[i + 2, :, 0:chan] = pltpu.roll(g, 2, 0).astype(BF16)
            gtaps[i + 2, :, chan:2 * chan] = pltpu.roll(g, 1, 0).astype(BF16)
            gtaps[i + 2, :, 2 * chan:] = g.astype(BF16)
        return carry

    lax.fori_loop(0, chunks, spread_grad, 0)

    def put_taps(row, a):
        taps[row, :, 0:chan] = pltpu.roll(a, 1, 0).astype(BF16)
        taps[row, :, chan:2 * chan] = a.astype(BF16)
        taps[row, :, 2 * chan:] = pltpu.roll(a, wide - 1, 0).astype(BF16)

    def spread_act(c, carry):
        for k in range(ROWS):
            i = c * ROWS + k
            put_taps(i + 1, widen(silu(x_in[i].astype(F32))))
        return carry

    lax.fori_loop(0, chunks, spread_act, 0)

    taps[0] = zero_row
    taps[side + 1] = zero_row
    pl.semaphore_wait(barrier, n_sp + n_dp - 2)
    pair_begin(fwd, fs, fr)

    acc[...] = jnp.zeros_like(acc)

    def kernel_chunk(c, carry):
        i0 = c * ROWS
        gt = gtaps[pl.ds(i0 + 2, ROWS), :, 2 * chan:].reshape(ROWS * wide, chan).T
        for r in range(3):
            acc[r] += jnp.dot(
                gt, taps[pl.ds(i0 + r, ROWS)].reshape(ROWS * wide, 3 * chan),
                preferred_element_type=F32)
        return carry

    lax.fori_loop(0, chunks, kernel_chunk, 0)
    pair_relay(fwd, fs, fr)
    pair_finish(fwd, fs, fr)

    def near(buf, e):
        return buf[adj[0, 0, e], adj[0, 1, e]]

    def near_corner(buf, k, row):
        return buf[adj[0, 0, 4 + k], adj[0, 1, 4 + k]].astype(F32)[row:row + 1]

    corner = [near_corner(fwd, k, 0) for k in range(4)]

    def rim_row(v, behind, ahead):
        return jnp.where(r64 < side, v, jnp.where(r64 == side, behind, jnp.where(r64 == wide - 1, ahead, 0.0)))

    put_taps(0, rim_row(flip(near(fwd, 0)), corner[1], corner[0]))
    put_taps(side + 1, rim_row(near(fwd, 2).astype(F32), corner[2], corner[3]))
    col_a[...] = near(fwd, 3).astype(F32)
    col_b[...] = flip(near(fwd, 1))

    def turned(v):
        return v.astype(BF16).T

    acc[0] += jnp.dot(turned(gtaps[2, :, 2 * chan:]), taps[0], preferred_element_type=F32)
    acc[2] += jnp.dot(turned(gtaps[side + 1, :, 2 * chan:]), taps[side + 1], preferred_element_type=F32)
    for e, rim in ((0, col_a), (1, col_b)):
        gt = turned(col_g[e])
        at = 2 * e * chan
        for r, turn in ((0, 1), (1, 0), (2, wide - 1)):
            v = pltpu.roll(rim[...], turn, 0) if turn else rim[...]
            acc[r, :, at:at + chan] += jnp.dot(gt, v.astype(BF16), preferred_element_type=F32)
    for r in range(3):
        for c in range(3):
            at = (3 * r + c) * chan
            wgf[at:at + chan, :] = acc[r, :, c * chan:(c + 1) * chan].T
    size = parts.shape[1] - 16
    used = 9 * chan
    if n_sp * size > used:
        wgf[used:, :] = jnp.zeros((n_sp * size - used, chan), F32)

    def scatter_copy(k):
        peer, dev = at_sp(k)
        src = wg.at[peer]
        start = pltpu.make_async_remote_copy(
            src_ref=src, dst_ref=parts.at[me], send_sem=ss.at[peer],
            recv_sem=sr.at[me], device_id=dev, device_id_type=MESH)
        wait = pltpu.make_async_remote_copy(
            src_ref=src, dst_ref=parts.at[peer], send_sem=ss.at[peer],
            recv_sem=sr.at[peer], device_id=dev, device_id_type=MESH)
        return start, wait

    def own_rows(peer):
        return wgf[pl.ds(pl.multiple_of(peer * size, 16), size), :]

    def scatter_start(k, c):
        peer = lax.rem(me + k, n_sp)
        wg[peer] = encode(own_rows(peer))
        scatter_copy(k)[0].start()
        return c

    def scatter_wait(k, c):
        scatter_copy(k)[1].wait()
        return c

    lax.fori_loop(1, n_sp, scatter_start, 0)
    parts[me] = encode(own_rows(me))

    s16 = lax.broadcasted_iota(jnp.int32, (ROWS, 16, chan), 1)
    at_right = (side - 1) // 16 * 16
    for c in range(chunks):
        lo = c * ROWS
        v = taps[lo + 1:lo + 1 + ROWS, 0:16, 0:chan].astype(F32)
        v = jnp.where(s16 == 0, col_a[lo:lo + ROWS, :][:, None, :], v)
        taps[lo + 1:lo + 1 + ROWS, 0:16, 0:chan] = v.astype(BF16)
        v = taps[lo + 1:lo + 1 + ROWS, at_right:at_right + 16, 2 * chan:].astype(F32)
        v = jnp.where(s16 == side - 1 - at_right, col_b[lo:lo + ROWS, :][:, None, :], v)
        taps[lo + 1:lo + 1 + ROWS, at_right:at_right + 16, 2 * chan:] = v.astype(BF16)


    def grad_rows(first, count):
        total = jnp.zeros((count * wide, chan), F32)
        for r in range(3):
            total += jnp.dot(
                gtaps[pl.ds(first + r, count)].reshape(count * wide, 3 * chan), wt[r],
                preferred_element_type=F32)
        pad_grad[pl.ds(first, count)] = total.reshape(count, wide, chan)

    def grad_chunk(c, carry):
        grad_rows(c * ROWS, ROWS)
        return carry

    lax.fori_loop(0, chunks, grad_chunk, 0)
    grad_rows(side, 2)

    for c in range(chunks):
        lo = c * ROWS
        col_a[lo:lo + ROWS, :] = column(pad_grad[lo + 1:lo + 1 + ROWS, 0:8, :], 0)
        col_b[lo:lo + ROWS, :] = column(pad_grad[lo + 1:lo + 1 + ROWS, side:side + 8, :], 1)
    first_row = pad_grad[0]
    last_row = pad_grad[side + 1]
    top = pltpu.roll(first_row, wide - 1, 0)
    bottom = pltpu.roll(last_row, wide - 1, 0)

    def pack(v, corner):
        return jnp.where(r64 < side, v, jnp.where(r64 == side, corner, 0.0)).astype(BF16)

    back[me, 0] = pack(top, first_row[0:1])
    back[me, 1] = pack(col_b[...], first_row[side + 1:side + 2])
    back[me, 2] = pack(flip(bottom.astype(BF16)), last_row[side + 1:side + 2])
    back[me, 3] = pack(flip(col_a[...].astype(BF16)), last_row[0:1])

    pair_begin(back, bs, br)

    lax.fori_loop(1, n_sp, scatter_wait, 0)
    mine = lax.fori_loop(0, n_sp, lambda k, t: t + decode(parts[k]), jnp.zeros((size, chan), F32))
    dps[my_dp] = encode(mine)
    begin(dps, my_dp, n_dp, at_dp, ds_, dr)

    def conv_chunk(c, carry):
        i0 = c * ROWS
        total = jnp.zeros((ROWS * wide, chan), F32)
        for r in range(3):
            total += jnp.dot(
                taps[pl.ds(i0 + r, ROWS)].reshape(ROWS * wide, 3 * chan), w_in[r],
                preferred_element_type=F32)
        conv = total.reshape(ROWS, wide, chan)[:, :side, :]
        field = x_in[pl.ds(i0, ROWS)].astype(F32)
        out[pl.ds(i0, ROWS)] = (field + conv + bias[...].reshape(1, 1, chan)).astype(BF16)
        return carry

    lax.fori_loop(0, chunks, conv_chunk, 0)
    out_copy = pltpu.make_async_copy(out, out_hbm, lo_sem.at[0])
    out_copy.start()

    pair_relay(back, bs, br)

    finish(dps, my_dp, n_dp, at_dp, ds_, dr)
    total = decode(dps[0])
    for d in range(1, n_dp):
        total = total + decode(dps[d])
    full[me] = encode(total)
    begin(full, me, n_sp, at_sp, gs, gr)

    pair_finish(back, bs, br)

    def inner(v):
        return jnp.where(r64 < side, v, 0.0)

    ends = [near_corner(back, k, side) for k in range(4)]
    pad_grad[1] += pltpu.roll(inner(flip(near(back, 0))), 1, 0)
    pad_grad[side] += pltpu.roll(inner(near(back, 2).astype(F32)), 1, 0)
    col_a[...] = inner(near(back, 3).astype(F32)) + jnp.where(r64 == 0, ends[0], jnp.where(r64 == side - 1, ends[3], 0.0))
    col_b[...] = inner(flip(near(back, 1))) + jnp.where(r64 == 0, ends[1], jnp.where(r64 == side - 1, ends[2], 0.0))

    r56 = lax.broadcasted_iota(jnp.int32, (side, chan), 0)

    def finish_rows(c, carry):
        for k in range(ROWS):
            i = c * ROWS + k
            p = pltpu.roll(pad_grad[i + 1], wide - 1, 0)[:side]
            p = p + jnp.where(r56 == 0, col_a[pl.ds(i, 1), :], jnp.where(r56 == side - 1, col_b[pl.ds(i, 1), :], 0.0))
            v = x_in[i].astype(F32)
            s = 1.0 / (1.0 + jnp.exp(-v))
            gin_out[i] = (g_in[i].astype(F32) + p * s * (1.0 + v * (1.0 - s))).astype(BF16)
        return carry

    lax.fori_loop(0, chunks, finish_rows, 0)
    gin_copy = pltpu.make_async_copy(gin_out, gin_hbm, lo_sem.at[1])
    gin_copy.start()

    finish(full, me, n_sp, at_sp, gs, gr)
    kernel_copy = pltpu.make_async_copy(full, wg_out, lo_sem.at[2])
    kernel_copy.start()
    kernel_copy.wait()
    gin_copy.wait()
    out_copy.wait()


def hand_on(a_in, codes_in, c_in, a_out, wg_out, c_out, a, codes, c, wgf, sems):
    first = pltpu.make_async_copy(codes_in, codes, sems.at[0])
    loads = [pltpu.make_async_copy(a_in, a, sems.at[1]), pltpu.make_async_copy(c_in, c, sems.at[2])]
    stores = [pltpu.make_async_copy(a, a_out, sems.at[3]), pltpu.make_async_copy(c, c_out, sems.at[4])]
    used = wg_out.shape[0]
    n_sp, rows = codes.shape[0], codes.shape[1]
    size = rows - 16
    last = pltpu.make_async_copy(wgf.at[pl.ds(0, used)], wg_out, sems.at[5])
    first.start()
    for one in loads:
        one.start()
    first.wait()

    def open_rows(k, carry):
        wgf[pl.ds(pl.multiple_of(k * size, 16), size), :] = decode(codes[k])
        return carry

    lax.fori_loop(0, n_sp, open_rows, 0)
    last.start()
    for load, store in zip(loads, stores):
        load.wait()
        store.start()
    for one in stores:
        one.wait()
    last.wait()


def per_device(n_sp, n_dp, block_in, weights, out_bias, adjacency, cotangent):
    side, chan = block_in.shape[2], block_in.shape[4]
    wide = wide_of(side)
    size = -(-9 * chan // (16 * n_sp)) * 16
    vmem = pl.BlockSpec(memory_space=pltpu.VMEM)
    hbm = pl.BlockSpec(memory_space=pl.ANY)
    sem = pltpu.SemaphoreType.DMA
    shapes = (
        jax.ShapeDtypeStruct((side, side, chan), BF16),
        jax.ShapeDtypeStruct((9 * chan, chan), F32),
        jax.ShapeDtypeStruct((side, side, chan), BF16),
    )
    codes = jax.ShapeDtypeStruct((n_sp, size + 16, chan), jnp.int16)
    held = pl.pallas_call(
        functools.partial(block_kernel, n_sp, n_dp, side),
        out_shape=(shapes[0], codes, shapes[2]),
        in_specs=[pl.BlockSpec(memory_space=pltpu.SMEM), vmem, vmem, vmem, vmem],
        out_specs=(hbm, hbm, hbm),
        scratch_shapes=[
            pltpu.VMEM((side + 2, wide, 3 * chan), BF16),
            pltpu.VMEM((side + 4, wide, 3 * chan), BF16),
            pltpu.VMEM((side + 2, wide, chan), F32),
            pltpu.VMEM((3, 3 * chan, chan), BF16),
            pltpu.VMEM((3, chan, 3 * chan), F32),
            pltpu.VMEM((wide, chan), F32),
            pltpu.VMEM((wide, chan), F32),
            pltpu.VMEM((n_sp, 4, wide, chan), BF16),
            pltpu.VMEM((n_sp, 4, wide, chan), BF16),
            pltpu.VMEM((n_sp, size + 16, chan), jnp.int16),
            pltpu.VMEM((n_sp, size + 16, chan), jnp.int16),
            pltpu.VMEM((n_dp, size + 16, chan), jnp.int16),
            pltpu.VMEM((n_sp, size + 16, chan), jnp.int16),
            sem((n_sp,)), sem((n_sp,)), sem((n_sp,)), sem((n_sp,)), sem((n_sp,)), sem((n_sp,)),
            sem((n_dp,)), sem((n_dp,)), sem((n_sp,)), sem((n_sp,)),
            pltpu.VMEM((side, side, chan), BF16),
            pltpu.VMEM((side, side, chan), BF16),
            pltpu.VMEM((n_sp * size, chan), F32),
            sem((3,)),
            pltpu.VMEM((2, wide, chan), F32),
        ],
        compiler_params=pltpu.CompilerParams(
            collective_id=0, has_side_effects=True, vmem_limit_bytes=56 * 2**20),
    )(
        adjacency.transpose(0, 2, 1), block_in[0, 0], weights.reshape(3, 3 * chan, chan), out_bias.reshape(1, chan),
        cotangent[0, 0],
    )
    result, wgrad, grad_in = pl.pallas_call(
        hand_on,
        out_shape=shapes,
        in_specs=[hbm, hbm, hbm],
        out_specs=(hbm, hbm, hbm),
        scratch_shapes=[pltpu.VMEM(one.shape, one.dtype) for one in (shapes[0], codes, shapes[2])] + [pltpu.VMEM((n_sp * size, chan), F32), sem((6,))],
    )(*held)
    return (result[None, None], wgrad.reshape(weights.shape), grad_in[None, None])


def solution(mesh):
    placed = (
        P("dp", "space", None, None, None),
        P(),
        P(),
        P("space", None, None),
        P("dp", "space", None, None, None),
    )
    return jax.shard_map(
        functools.partial(per_device, mesh.shape["space"], mesh.shape["dp"]),
        mesh=mesh,
        in_specs=placed,
        out_specs=(P("dp", "space", None, None, None), P(), P("dp", "space", None, None, None)),
        check_vma=False,
    )
```
